768 devices in a mesh: grp: 24 (over z, core), sub: 32 (over x, y).
Axes of the slice: x: 4, y: 8, z: 12, core: 2. Of those that a mesh axis runs over, the one named last changes fastest.
Arguments:
- residual4: float32 [128, 96, 128], P(None, 'grp', 'sub'), may hold values from -6 to 6
- spacing: float32 [128], replicated, may hold values from 0.5 to 2
Outputs:
- correction: float32 [128, 96, 128], P(None, 'grp', 'sub')
- coarse_solution: float32 [64, 48, 64], P(None, 'grp', 'sub')
The draws below stay inside these ranges and needn't reach their ends.
All inputs are finite; a program needn't handle non-finite values.
Results may differ from the reference program's by a relative error of at most 0.00026.
Values sent between devices are 32-bit elements; how exact they have to be, the bound alone decides.
A program may use at most 64 MiB of HBM per device.

```python
import math
import jax
import jax.numpy as jnp
from jax import lax

NZ = 128
SWEEPS = 2
NX4 = 128
NY4 = 96


def block_scale(own_key, shape, cuts, low, largest):
    gain, own = 1.0, jax.random.fold_in(own_key, 6)
    for position, shards_of in cuts:
        heights = jnp.exp(jax.random.uniform(jax.random.fold_in(own, position), (shards_of,), jnp.float32, low / len(cuts), largest / len(cuts)))
        gain = gain * jnp.repeat(heights, shape[position] // shards_of).reshape([-1 if axis == position else 1 for axis in range(len(shape))])
    return gain


def scatter_about(key, dims, deviation, reach, cuts=(), kind=jnp.bfloat16):
    level = block_scale(key, dims, cuts, -0.22, 0.18) if cuts else 1.0
    array = jax.random.normal(key, dims, jnp.float32) * deviation * level
    return jnp.minimum(jnp.maximum(array, -reach), reach).astype(kind)


def setup_inputs(seed: int = 0) -> dict:
    seeds = jax.random.split(jax.random.key(seed), 3)
    return {
        "residual4": scatter_about(seeds[0], (NZ, NY4, NX4), 1.0, 6.0, ((1, 24), (2, 32)), jnp.float32),
        "spacing": jnp.clip(jnp.exp(jax.random.uniform(seeds[1], (NZ,), jnp.float32, math.log(0.5), math.log(2.0))), 0.5, 2.0),
    }


def couplings(spacing):
    face_coef = 2.0 / (spacing[:-1] + spacing[1:])
    zero_end = jnp.zeros((1,), spacing.dtype)
    upper_face = jnp.concatenate([face_coef, zero_end])
    lower_face = jnp.concatenate([zero_end, face_coef])
    return upper_face, lower_face


def column(vector):
    return vector[:, None, None]


def operator(grid_field, spacing, upper_face, lower_face, plane_scale):
    west_side = jnp.roll(grid_field, 1, 2)
    east_side = jnp.roll(grid_field, -1, 2)
    south_side = jnp.roll(grid_field, 1, 1)
    north_side = jnp.roll(grid_field, -1, 1)
    zero_layer = jnp.zeros_like(grid_field[:1])
    above_cell = jnp.concatenate([grid_field[1:], zero_layer], 0)
    below_cell = jnp.concatenate([zero_layer, grid_field[:-1]], 0)
    inplane = plane_scale * column(spacing) * (4.0 * grid_field - west_side - east_side - south_side - north_side)
    vertical = column(upper_face) * (grid_field - above_cell) + column(lower_face) * (grid_field - below_cell)
    return inplane + vertical


def solve_columns(real_part, imag_part, spacing5, eigen_xy, anchor):
    upper5, lower5 = couplings(spacing5)
    levels_z = spacing5.shape[0]
    bottom_flag = (jnp.arange(levels_z) == 0).astype(real_part.dtype)
    source = jnp.stack([real_part, imag_part], 1)

    def forward(carry_in, inputs):
        factor_prev, value_prev = carry_in
        height, coef_up, coef_low, flag_k, rhs_k = inputs
        pivot = eigen_xy * height + coef_up + coef_low + flag_k * anchor + coef_low * factor_prev
        factor_k = -coef_up / pivot
        value_k = (rhs_k + coef_low * value_prev) / pivot
        return (factor_k, value_k), (factor_k, value_k)

    start_state = (jnp.zeros_like(eigen_xy), jnp.zeros_like(source[0]))
    unused, (factors, values) = lax.scan(forward, start_state, (spacing5, upper5, lower5, bottom_flag, source))

    def backward(next_cell, inputs):
        factor_k, value_k = inputs
        solved_k = value_k - factor_k * next_cell
        return solved_k, solved_k

    unused_last, solved = lax.scan(backward, jnp.zeros_like(source[0]), (factors, values), reverse=True)
    return solved[:, 0], solved[:, 1]


def reference(residual4, spacing):
    damping = 0.8
    upper_face, lower_face = couplings(spacing)
    diagonal = column(4.0 * spacing + upper_face + lower_face)
    smooth = damping * residual4 / diagonal
    for sweep_no in range(SWEEPS - 1):
        smooth = smooth + damping * (residual4 - operator(smooth, spacing, upper_face, lower_face, 1.0)) / diagonal
    leftover = residual4 - operator(smooth, spacing, upper_face, lower_face, 1.0)
    levels_z, rows_y, cols_x = leftover.shape
    coarse = leftover.reshape(levels_z // 2, 2, rows_y // 2, 2, cols_x // 2, 2).sum(axis=(1, 3, 5)) / 4.0
    spectrum = jnp.fft.fft2(coarse, axes=(1, 2))
    mean_mode = jnp.mean(spectrum[:, 0, 0])
    spectrum = spectrum.at[:, 0, 0].add(-mean_mode)
    real_part = jnp.real(spectrum).astype(coarse.dtype)
    imag_part = jnp.imag(spectrum).astype(coarse.dtype)
    ny5 = rows_y // 2
    nx5 = cols_x // 2
    wave_y = jnp.arange(ny5).astype(coarse.dtype)
    wave_x = jnp.arange(nx5).astype(coarse.dtype)
    eigen_xy = 0.25 * ((2.0 - 2.0 * jnp.cos(2.0 * math.pi * wave_x[None, :] / nx5)) + (2.0 - 2.0 * jnp.cos(2.0 * math.pi * wave_y[:, None] / ny5)))
    anchor = ((jnp.arange(ny5)[:, None] == 0) & (jnp.arange(nx5)[None, :] == 0)).astype(coarse.dtype)
    spacing5 = spacing.reshape(levels_z // 2, 2).sum(axis=1)
    solved_re, solved_im = solve_columns(real_part, imag_part, spacing5, eigen_xy, anchor)
    coarse_solution = jnp.real(jnp.fft.ifft2(solved_re + 1j * solved_im, axes=(1, 2))).astype(coarse.dtype)
    lifted = smooth + jnp.repeat(jnp.repeat(jnp.repeat(coarse_solution, 2, 0), 2, 1), 2, 2)
    for sweep_no in range(SWEEPS):
        lifted = lifted + damping * (residual4 - operator(lifted, spacing, upper_face, lower_face, 1.0)) / diagonal
    return lifted, coarse_solution
```

```python
import functools
import math

import jax
import jax.numpy as jnp
from jax import lax
from jax.experimental import pallas as pl
from jax.experimental.pallas import tpu as pltpu
from jax.sharding import PartitionSpec as P

MESH = pl.DeviceIdType.MESH
HIGHEST = lax.Precision.HIGHEST
DAMPING = 0.8
LANES = 128
HALF = 64


def matmul(left, right):
    return lax.dot_general(
        left, right, (((1,), (0,)), ((), ())), precision=HIGHEST, preferred_element_type=jnp.float32
    )


def iota(shape, axis):
    return lax.broadcasted_iota(jnp.int32, shape, axis).astype(jnp.float32)


def wrapped(value, count):
    return value - count * jnp.floor((value + 0.5) * (1.0 / count))


def cos_turn(step, count):
    step = jnp.minimum(step, count - step)
    flip = step > count / 4
    step = jnp.where(flip, count / 2 - step, step)
    angle = step * (2.0 * math.pi / count)
    sq = angle * angle
    total = jnp.full_like(sq, 1.0 / math.factorial(16))
    for power in range(14, -1, -2):
        sign = 1.0 if power % 4 == 0 else -1.0
        total = total * sq + sign / math.factorial(power)
    return jnp.where(flip, -total, total)


def up_z(field):
    return pltpu.roll(field, LANES - 1, axis=field.ndim - 1)


def down_z(field):
    return pltpu.roll(field, 1, axis=field.ndim - 1)


def operate(rows, south, north, coef):
    height, upper, lower, diagonal = coef
    span = rows.shape[1]
    west = pltpu.roll(rows, 1, axis=1)
    east = pltpu.roll(rows, span - 1, axis=1)
    sides = (west + east) + (south + north)
    return diagonal * rows - height * sides - upper * up_z(rows) - lower * down_z(rows)


def kernel(
    n_grp, n_sub,
    res_ref, spacing_ref, cor_ref, coarse_ref,
    pad, table, msg1, recv1, msg2, recv2, msg3, recv3, halo, big, smooth_ref, pairs,
    scale_r, scale_p, scale_q,
    halo_send, halo_recv, send1, got1, send2, got2, send3, got3,
):
    me_g = lax.axis_index("grp")
    me_s = lax.axis_index("sub")
    ny5, nx5 = 2 * n_grp, 2 * n_sub

    def grp_at(k):
        return lax.rem(me_g + k, n_grp)

    def sub_at(k):
        return lax.rem(me_s + k, n_sub)

    ring = [(a, b) for a in (0, 1, n_grp - 1) for b in (0, 1, n_sub - 1) if (a, b) != (0, 0)]
    barrier = pltpu.get_barrier_semaphore()

    def greet_grp(k, carry):
        pl.semaphore_signal(barrier, inc=1, device_id=(grp_at(k), me_s), device_id_type=MESH)
        return carry

    def greet_sub(k, carry):
        pl.semaphore_signal(barrier, inc=1, device_id=(me_g, sub_at(k)), device_id_type=MESH)
        return carry

    lax.fori_loop(1, n_grp, greet_grp, 0)
    lax.fori_loop(1, n_sub, greet_sub, 0)
    for a, b in ring:
        if a and b:
            pl.semaphore_signal(
                barrier, inc=1, device_id=(grp_at(a), sub_at(b)), device_id_type=MESH
            )

    lane = lax.broadcasted_iota(jnp.int32, (8, LANES), 1)
    height8 = jnp.broadcast_to(spacing_ref[...], (8, LANES))
    face = 2.0 / (height8 + up_z(height8))
    upper8 = jnp.where(lane < LANES - 1, face, 0.0)
    lower8 = jnp.where(lane > 0, down_z(face), 0.0)
    diag8 = 4.0 * height8 + upper8 + lower8
    damp8 = DAMPING / diag8
    coef8 = (height8[None], upper8[None], lower8[None], diag8[None])

    pad[...] = jnp.zeros_like(pad)
    pad[2:6, 2:6, :] = res_ref[...]
    block = pad[...]
    zero_row = jnp.zeros((1, 8, LANES), jnp.float32)

    def operate_zero(rows):
        south = jnp.concatenate([zero_row, rows[:-1]], 0)
        north = jnp.concatenate([rows[1:], zero_row], 0)
        return operate(rows, south, north, coef8)

    first = damp8[None] * block
    second = first + damp8[None] * (block - operate_zero(first))
    leftover = block - operate_zero(second)
    row_pairs = jnp.concatenate([leftover[2 * j] + leftover[2 * j + 1] for j in range(4)], 0)
    z_in = lax.broadcasted_iota(jnp.int32, (LANES, LANES), 0)
    z_out = lax.broadcasted_iota(jnp.int32, (LANES, LANES), 1)
    gather_z = jnp.where((z_in >> 1) == (z_out & (HALF - 1)), 1.0, 0.0)
    pairs[...] = matmul(row_pairs, 0.25 * gather_z)
    parts = pairs[pl.ds(0, 16, stride=2), :] + pairs[pl.ds(1, 16, stride=2), :]

    shape_t = (n_grp, LANES)
    owner = lax.broadcasted_iota(jnp.int32, shape_t, 0) + me_g
    owner = jnp.where(owner >= n_grp, owner - n_grp, owner).astype(jnp.float32)
    second_half = lax.broadcasted_iota(jnp.int32, shape_t, 1) >= HALF
    alone = owner == 0.0
    wave = jnp.where(alone & second_half, 1.0 * n_grp, owner)
    shift = jnp.where(second_half & jnp.logical_not(alone), 0.25 * ny5, 0.0)
    for j in range(4):
        row = wrapped((2 * me_g + (j - 1)).astype(jnp.float32), ny5)
        table[j] = cos_turn(wrapped(wave * row - shift, ny5), ny5)

    for k in range(n_grp):
        total = table[0, k : k + 1, :] * parts[0:4]
        for j in range(1, 4):
            total = total + table[j, k : k + 1, :] * parts[4 * j : 4 * j + 4]
        if k == 0:
            recv1[0] = total
        else:
            msg1[k] = total

    pl.semaphore_wait(barrier, n_grp + n_sub - 2 + 4)

    def send_1(k, carry):
        pltpu.make_async_remote_copy(
            src_ref=msg1.at[k], dst_ref=recv1.at[k], send_sem=send1, recv_sem=got1,
            device_id=(grp_at(k), me_s), device_id_type=MESH,
        ).start()
        return carry

    lax.fori_loop(1, n_grp, send_1, 0)
    for place, (a, b) in enumerate(ring):
        pltpu.make_async_remote_copy(
            src_ref=res_ref, dst_ref=halo.at[place], send_sem=halo_send, recv_sem=halo_recv,
            device_id=(grp_at(a), sub_at(b)), device_id_type=MESH,
        ).start()

    lane_m = lax.broadcasted_iota(jnp.int32, (nx5, LANES), 1)
    row_m = lax.broadcasted_iota(jnp.int32, (nx5, LANES), 0)
    z5 = lane_m & (HALF - 1)
    height5 = matmul(height8, gather_z)
    face5 = 2.0 / (height5 + up_z(height5))
    z5_8 = lane & (HALF - 1)
    upper5 = jnp.where(z5_8 < HALF - 1, face5, 0.0)[0:1]
    lower5 = jnp.where(z5_8 > 0, down_z(face5), 0.0)[0:1]
    height5 = height5[0:1]
    mode = row_m.astype(jnp.float32)
    wave_x = jnp.where(mode > n_sub, mode - n_sub, mode)
    sin_x = cos_turn(n_sub - wave_x, 2 * nx5)
    me_gf = me_g.astype(jnp.float32)
    half_m = lane_m >= HALF
    wave_y = jnp.where(half_m, jnp.where(me_gf == 0.0, 1.0 * n_grp, me_gf), me_gf)
    sin_y = cos_turn(n_grp - wave_y, 2 * ny5)
    lam = sin_x * sin_x + sin_y * sin_y
    still = (row_m == 0) & (wave_y == 0.0)
    anchor = jnp.where(still & (z5 == 0), 1.0, 0.0)
    excess = lam * height5 + anchor
    inverse = 1.0 / (excess + upper5 + lower5)
    below = lower5 * inverse
    above = upper5 * inverse
    excess = excess * inverse
    first_scale = inverse
    weight = jnp.where(me_gf == 0.0, 1.0 / ny5, 2.0 / ny5)
    for level in range(6):
        step = 1 << level
        below_dn = pltpu.roll(below, step, axis=1)
        above_up = pltpu.roll(above, LANES - step, axis=1)
        excess_dn = pltpu.roll(excess, step, axis=1)
        excess_up = pltpu.roll(excess, LANES - step, axis=1)
        inverse = 1.0 / (excess + below * (below_dn + excess_dn) + above * (above_up + excess_up))
        low, high = below * inverse, above * inverse
        last = weight if level == 5 else 1.0
        scale_r[level] = inverse * last
        scale_p[level] = low * last
        scale_q[level] = high * last
        excess = excess * inverse + low * excess_dn + high * excess_up
        below, above = low * below_dn, high * above_up

    shape_f = (nx5, 4 * n_sub)
    mode_f, col_f = iota(shape_f, 0), iota(shape_f, 1)
    place_f = jnp.floor((col_f + 0.5) * 0.25)
    column_f = wrapped(2.0 * place_f + (col_f - 4.0 * place_f) - 1.0, nx5)
    odd_f = mode_f > n_sub
    phase_f = jnp.where(odd_f, mode_f - n_sub, mode_f) * column_f - jnp.where(odd_f, 0.25 * nx5, 0.0)
    forward_x = cos_turn(wrapped(phase_f, nx5), nx5)
    shape_b = (8, nx5)
    mode_b, col_b = iota(shape_b, 1), iota(shape_b, 0) - 1.0
    odd_b = mode_b > n_sub
    phase_b = jnp.where(odd_b, mode_b - n_sub, mode_b) * col_b - jnp.where(odd_b, 0.25 * nx5, 0.0)
    once = (mode_b == 0.0) | (mode_b == 1.0 * n_sub)
    backward_x = cos_turn(wrapped(phase_b, nx5), nx5) * jnp.where(once, 1.0 / nx5, 2.0 / nx5)

    pltpu.make_async_copy(recv1.at[pl.ds(1, n_grp - 1)], recv1.at[pl.ds(1, n_grp - 1)], got1).wait()
    own = jnp.sum(recv1[...], axis=0)
    msg2[...] = own
    recv2[0] = own

    def send_2(k, carry):
        pltpu.make_async_remote_copy(
            src_ref=msg2, dst_ref=recv2.at[n_sub - k], send_sem=send2, recv_sem=got2,
            device_id=(me_g, sub_at(k)), device_id_type=MESH,
        ).start()
        return carry

    lax.fori_loop(1, n_sub, send_2, 0)
    pltpu.make_async_copy(recv2.at[pl.ds(1, n_sub - 1)], recv2.at[pl.ds(1, n_sub - 1)], got2).wait()

    rows_in = jnp.concatenate([recv2[k] for k in range(n_sub)], 0)
    field = matmul(forward_x, rows_in)
    mean = jnp.sum(jnp.where(still, field, 0.0)) * (1.0 / HALF)
    field = jnp.where(still, field - mean, field) * first_scale
    for level in range(6):
        step = 1 << level
        field = (
            scale_r[level] * field
            + scale_p[level] * pltpu.roll(field, step, axis=1)
            + scale_q[level] * pltpu.roll(field, LANES - step, axis=1)
        )
    back = matmul(backward_x, field)[0:4]
    msg3[...] = back
    recv3[0] = back

    def send_3(k, carry):
        pltpu.make_async_remote_copy(
            src_ref=msg3, dst_ref=recv3.at[n_grp - k], send_sem=send3, recv_sem=got3,
            device_id=(grp_at(k), me_s), device_id_type=MESH,
        ).start()
        return carry

    lax.fori_loop(1, n_grp, send_3, 0)

    pltpu.make_async_copy(halo, halo, halo_recv).wait()
    big[:, 12:16, :] = jnp.zeros((12, 4, LANES), jnp.float32)
    big[4:8, 4:8, :] = res_ref[...]
    for place, (a, b) in enumerate(ring):
        at_y = {0: 4, 1: 0, n_grp - 1: 8}[a]
        at_x = {0: 4, 1: 0, n_sub - 1: 8}[b]
        big[at_y : at_y + 4, at_x : at_x + 4, :] = halo[place]
    wide = big[...]
    coef1 = tuple(value[:, 0:1] for value in coef8)
    damp1 = damp8[None, 0:1]
    first_w = damp1 * wide
    inner = first_w[1:-1] + damp1 * (
        wide[1:-1] - operate(first_w[1:-1], first_w[:-2], first_w[2:], coef1)
    )
    smooth_ref[...] = inner[1:-1]
    smooth = smooth_ref[:, 2:10, :]
    near = big[2:10, 2:10, :]

    pltpu.make_async_copy(recv3.at[pl.ds(1, n_grp - 1)], recv3.at[pl.ds(1, n_grp - 1)], got3).wait()
    for j in range(4):
        total = table[j, 0:1, :] * recv3[0]
        for k in range(1, n_grp):
            total = total + table[j, k : k + 1, :] * recv3[k]
        if j in (1, 2):
            folded = total + pltpu.roll(total, HALF, axis=1)
            coarse_ref[j - 1] = folded[1:3, 0:HALF]
        pairs[pl.ds(8 * j, 4, stride=2), :] = total
        pairs[pl.ds(8 * j + 1, 4, stride=2), :] = total
    spread_z = jnp.where((z_out >> 1) == (z_in & (HALF - 1)), 1.0, 0.0)
    coarse = matmul(pairs[...], spread_z)
    lifted = smooth + jnp.concatenate(
        [coarse[8 * (j // 2) : 8 * (j // 2) + 8][None] for j in range(8)], 0
    )
    lifted = lifted[1:-1] + damp8[None] * (
        near[1:-1] - operate(lifted[1:-1], lifted[:-2], lifted[2:], coef8)
    )
    lifted = lifted[1:-1] + damp8[None] * (
        near[2:-2] - operate(lifted[1:-1], lifted[:-2], lifted[2:], coef8)
    )
    cor_ref[...] = lifted[:, 2:6, :]

    pltpu.make_async_copy(halo, halo, halo_send).wait()
    pltpu.make_async_copy(recv1.at[pl.ds(1, n_grp - 1)], recv1.at[pl.ds(1, n_grp - 1)], send1).wait()
    pltpu.make_async_copy(recv2.at[pl.ds(1, n_sub - 1)], recv2.at[pl.ds(1, n_sub - 1)], send2).wait()
    pltpu.make_async_copy(recv3.at[pl.ds(1, n_grp - 1)], recv3.at[pl.ds(1, n_grp - 1)], send3).wait()


def on_device(n_grp, n_sub, residual4, spacing):
    f32 = jnp.float32
    nx5 = 2 * n_sub
    dma = pltpu.SemaphoreType.DMA
    vmem = pl.BlockSpec(memory_space=pltpu.VMEM)
    correction, coarse = pl.pallas_call(
        functools.partial(kernel, n_grp, n_sub),
        out_shape=(
            jax.ShapeDtypeStruct((4, 4, LANES), f32),
            jax.ShapeDtypeStruct((2, 2, HALF), f32),
        ),
        in_specs=[vmem, vmem],
        out_specs=(vmem, vmem),
        scratch_shapes=[
            pltpu.VMEM((8, 8, LANES), f32),
            pltpu.VMEM((4, n_grp, LANES), f32),
            pltpu.VMEM((n_grp, 4, LANES), f32),
            pltpu.VMEM((n_grp, 4, LANES), f32),
            pltpu.VMEM((4, LANES), f32),
            pltpu.VMEM((n_sub, 4, LANES), f32),
            pltpu.VMEM((4, LANES), f32),
            pltpu.VMEM((n_grp, 4, LANES), f32),
            pltpu.VMEM((8, 4, 4, LANES), f32),
            pltpu.VMEM((12, 16, LANES), f32),
            pltpu.VMEM((8, 16, LANES), f32),
            pltpu.VMEM((32, LANES), f32),
            pltpu.VMEM((6, nx5, LANES), f32),
            pltpu.VMEM((6, nx5, LANES), f32),
            pltpu.VMEM((6, nx5, LANES), f32),
        ]
        + [dma] * 8,
        compiler_params=pltpu.CompilerParams(collective_id=0, has_side_effects=True),
    )(jnp.transpose(residual4, (1, 2, 0)), spacing.reshape(1, LANES))
    return jnp.transpose(correction, (2, 0, 1)), jnp.transpose(coarse, (2, 0, 1))


def solution(mesh):
    placed = P(None, "grp", "sub")
    return jax.shard_map(
        functools.partial(on_device, mesh.shape["grp"], mesh.shape["sub"]),
        mesh=mesh,
        in_specs=(placed, P()),
        out_specs=(placed, placed),
        check_vma=False,
    )
```

```python
import functools
import math

import jax
import jax.numpy as jnp
from jax import lax
from jax.experimental import pallas as pl
from jax.experimental.pallas import tpu as pltpu
from jax.sharding import PartitionSpec as P

MESH = pl.DeviceIdType.MESH
HIGHEST = lax.Precision.HIGHEST
DAMPING = 0.8
LANES = 128
HALF = 64


def matmul(left, right):
    return lax.dot_general(
        left, right, (((1,), (0,)), ((), ())), precision=HIGHEST, preferred_element_type=jnp.float32
    )


def iota(shape, axis):
    return lax.broadcasted_iota(jnp.int32, shape, axis).astype(jnp.float32)


def wrapped(value, count):
    return value - count * jnp.floor((value + 0.5) * (1.0 / count))


def cos_turn(step, count):
    step = jnp.minimum(step, count - step)
    flip = step > count / 4
    step = jnp.where(flip, count / 2 - step, step)
    angle = step * (2.0 * math.pi / count)
    sq = angle * angle
    total = jnp.full_like(sq, 1.0 / math.factorial(16))
    for power in range(14, -1, -2):
        sign = 1.0 if power % 4 == 0 else -1.0
        total = total * sq + sign / math.factorial(power)
    return jnp.where(flip, -total, total)


def up_z(field):
    return pltpu.roll(field, LANES - 1, axis=field.ndim - 1)


def down_z(field):
    return pltpu.roll(field, 1, axis=field.ndim - 1)


def operate(rows, south, north, coef):
    height, upper, lower, diagonal = coef
    span = rows.shape[1]
    west = pltpu.roll(rows, 1, axis=1)
    east = pltpu.roll(rows, span - 1, axis=1)
    sides = (west + east) + (south + north)
    return diagonal * rows - height * sides - upper * up_z(rows) - lower * down_z(rows)


def torus(n_grp, n_sub):
    inner = 8 if n_sub % 8 == 0 else 2
    return (n_grp // 2, 2), (n_sub // inner, inner)


def offsets(sizes):
    outer, inner = sizes

    def hops(step):
        return min(step[0], outer - step[0]) + min(step[1], inner - step[1])

    steps = [(a, b) for a in range(outer) for b in range(inner) if (a, b) != (0, 0)]
    return sorted(steps, key=hops, reverse=True)


def kernel(
    n_grp, n_sub,
    res_hbm, spacing_hbm, cor_ref, coarse_ref,
    res_ref, spacing_ref, pad, table, msg1, recv1, msg2, recv2, msg3, recv3, halo, big, smooth_ref,
    pairs, scale_r, scale_p, scale_q,
    load1, load2, halo_send, halo_recv, send1, got1, send2, got2, send3, got3,
):
    me_g = lax.axis_index("grp")
    me_s = lax.axis_index("sub")
    ny5, nx5 = 2 * n_grp, 2 * n_sub
    grp_size, sub_size = torus(n_grp, n_sub)

    def moved(me, step, sizes):
        outer, inner = sizes
        high, low = me // inner, me % inner
        return ((high + step[0]) % outer) * inner + (low + step[1]) % inner

    def slot(step, sizes):
        outer, inner = sizes
        return (-step[0] % outer) * inner + (-step[1] % inner)

    grp_steps, sub_steps = offsets(grp_size), offsets(sub_size)
    ring = [(a, b) for a in (0, 1, n_grp - 1) for b in (0, 1, n_sub - 1) if (a, b) != (0, 0)]

    load_res = pltpu.make_async_copy(res_hbm, res_ref, load1)
    load_spacing = pltpu.make_async_copy(spacing_hbm, spacing_ref, load2)
    load_res.start()
    load_spacing.start()
    barrier = pltpu.get_barrier_semaphore()

    def greet(device):
        pl.semaphore_signal(barrier, inc=1, device_id=device, device_id_type=MESH)

    for place in range(max(len(grp_steps), len(sub_steps))):
        if place < len(grp_steps):
            greet((moved(me_g, grp_steps[place], grp_size), me_s))
        if place < len(sub_steps):
            greet((me_g, moved(me_s, sub_steps[place], sub_size)))
    for a, b in ring:
        if a and b:
            greet(((me_g + a) % n_grp, (me_s + b) % n_sub))

    shape_t = (n_sub, LANES)
    place_t = lax.broadcasted_iota(jnp.int32, shape_t, 0)
    outer, inner = sub_size
    high = me_s // inner + lax.shift_right_logical(place_t, inner.bit_length() - 1)
    low = me_s % inner + (place_t & (inner - 1))
    high = jnp.where(high >= outer, high - outer, high)
    low = jnp.where(low >= inner, low - inner, low)
    owner = (high * inner + low).astype(jnp.float32)
    second_half = lax.broadcasted_iota(jnp.int32, shape_t, 1) >= HALF
    alone = owner == 0.0
    wave = jnp.where(alone & second_half, 1.0 * n_sub, owner)
    shift = jnp.where(second_half & jnp.logical_not(alone), 0.25 * nx5, 0.0)
    for j in range(4):
        column = wrapped((2 * me_s + (j - 1)).astype(jnp.float32), nx5)
        table[j] = cos_turn(wrapped(wave * column - shift, nx5), nx5)

    load_spacing.wait()
    lane = lax.broadcasted_iota(jnp.int32, (8, LANES), 1)
    height8 = jnp.broadcast_to(spacing_ref[...], (8, LANES))
    face = 2.0 / (height8 + up_z(height8))
    upper8 = jnp.where(lane < LANES - 1, face, 0.0)
    lower8 = jnp.where(lane > 0, down_z(face), 0.0)
    diag8 = 4.0 * height8 + upper8 + lower8
    damp8 = DAMPING / diag8
    coef8 = (height8[None], upper8[None], lower8[None], diag8[None])

    pad[...] = jnp.zeros_like(pad)
    load_res.wait()
    pad[2:6, 2:6, :] = res_ref[...]
    block = pad[...]
    zero_row = jnp.zeros((1, 8, LANES), jnp.float32)

    def operate_zero(rows):
        south = jnp.concatenate([zero_row, rows[:-1]], 0)
        north = jnp.concatenate([rows[1:], zero_row], 0)
        return operate(rows, south, north, coef8)

    first = damp8[None] * block
    second = first + damp8[None] * (block - operate_zero(first))
    leftover = block - operate_zero(second)
    row_pairs = jnp.concatenate([leftover[2 * j] + leftover[2 * j + 1] for j in range(4)], 0)
    z_in = lax.broadcasted_iota(jnp.int32, (LANES, LANES), 0)
    z_out = lax.broadcasted_iota(jnp.int32, (LANES, LANES), 1)
    gather_z = jnp.where((z_in >> 1) == (z_out & (HALF - 1)), 1.0, 0.0)
    pairs[...] = matmul(row_pairs, 0.25 * gather_z)
    parts = [
        pairs[pl.ds(2 * j, 4, stride=8), :] + pairs[pl.ds(2 * j + 1, 4, stride=8), :]
        for j in range(4)
    ]
    for k in range(n_sub):
        total = table[0, k : k + 1, :] * parts[0]
        for j in range(1, 4):
            total = total + table[j, k : k + 1, :] * parts[j]
        if k == 0:
            recv1[0] = total
        else:
            msg1[k] = total

    pl.semaphore_wait(barrier, n_grp + n_sub - 2 + 4)

    for step in sub_steps:
        pltpu.make_async_remote_copy(
            src_ref=msg1.at[step[0] * inner + step[1]], dst_ref=recv1.at[slot(step, sub_size)],
            send_sem=send1, recv_sem=got1,
            device_id=(me_g, moved(me_s, step, sub_size)), device_id_type=MESH,
        ).start()

    lane_m = lax.broadcasted_iota(jnp.int32, (ny5, LANES), 1)
    row_m = lax.broadcasted_iota(jnp.int32, (ny5, LANES), 0)
    z5 = lane_m & (HALF - 1)
    height5 = matmul(height8, gather_z)
    face5 = 2.0 / (height5 + up_z(height5))
    z5_8 = lane & (HALF - 1)
    upper5 = jnp.where(z5_8 < HALF - 1, face5, 0.0)[0:1]
    lower5 = jnp.where(z5_8 > 0, down_z(face5), 0.0)[0:1]
    height5 = height5[0:1]
    mode = row_m.astype(jnp.float32)
    wave_y = jnp.where(mode > n_grp, mode - n_grp, mode)
    sin_y = cos_turn(n_grp - wave_y, 2 * ny5)
    me_sf = me_s.astype(jnp.float32)
    wave_x = jnp.where((lane_m >= HALF) & (me_sf == 0.0), 1.0 * n_sub, me_sf)
    sin_x = cos_turn(n_sub - wave_x, 2 * nx5)
    lam = sin_x * sin_x + sin_y * sin_y
    still = (row_m == 0) & (wave_x == 0.0)
    anchor = jnp.where(still & (z5 == 0), 1.0, 0.0)
    excess = lam * height5 + anchor
    inverse = 1.0 / (excess + upper5 + lower5)
    below = lower5 * inverse
    above = upper5 * inverse
    excess = excess * inverse
    first_scale = inverse
    weight = jnp.where(me_sf == 0.0, 1.0 / nx5, 2.0 / nx5)
    for level in range(6):
        step = 1 << level
        below_dn = pltpu.roll(below, step, axis=1)
        above_up = pltpu.roll(above, LANES - step, axis=1)
        excess_dn = pltpu.roll(excess, step, axis=1)
        excess_up = pltpu.roll(excess, LANES - step, axis=1)
        inverse = 1.0 / (excess + below * (below_dn + excess_dn) + above * (above_up + excess_up))
        low, high = below * inverse, above * inverse
        last = weight if level == 5 else 1.0
        scale_r[level] = inverse * last
        scale_p[level] = low * last
        scale_q[level] = high * last
        excess = excess * inverse + low * excess_dn + high * excess_up
        below, above = low * below_dn, high * above_up

    shape_f = (ny5, 4 * n_grp)
    mode_f, col_f = iota(shape_f, 0), iota(shape_f, 1)
    place_f = jnp.floor((col_f + 0.5) * 0.25)
    pair_f = jnp.floor((place_f + 0.5) * 0.5)
    side = 1.0 - 2.0 * (me_g % 2).astype(jnp.float32)
    row_f = 4.0 * pair_f + 2.0 * side * (place_f - 2.0 * pair_f) + (col_f - 4.0 * place_f) - 1.0
    odd_f = mode_f > n_grp
    phase_f = jnp.where(odd_f, mode_f - n_grp, mode_f) * wrapped(row_f, ny5)
    phase_f = phase_f - jnp.where(odd_f, 0.25 * ny5, 0.0)
    forward_y = cos_turn(wrapped(phase_f, ny5), ny5)
    shape_b = (8, ny5)
    mode_b, row_b = iota(shape_b, 1), iota(shape_b, 0) - 1.0
    odd_b = mode_b > n_grp
    phase_b = jnp.where(odd_b, mode_b - n_grp, mode_b) * row_b - jnp.where(odd_b, 0.25 * ny5, 0.0)
    once = (mode_b == 0.0) | (mode_b == 1.0 * n_grp)
    backward_y = cos_turn(wrapped(phase_b, ny5), ny5) * jnp.where(once, 1.0 / ny5, 2.0 / ny5)

    pltpu.make_async_copy(recv1.at[pl.ds(1, n_sub - 1)], recv1.at[pl.ds(1, n_sub - 1)], got1).wait()
    own = jnp.sum(recv1[...], axis=0)
    msg2[...] = own
    recv2[0] = own
    for step in grp_steps:
        pltpu.make_async_remote_copy(
            src_ref=msg2, dst_ref=recv2.at[slot(step, grp_size)], send_sem=send2, recv_sem=got2,
            device_id=(moved(me_g, step, grp_size), me_s), device_id_type=MESH,
        ).start()
    for place, (a, b) in enumerate(ring):
        pltpu.make_async_remote_copy(
            src_ref=res_ref, dst_ref=halo.at[place], send_sem=halo_send, recv_sem=halo_recv,
            device_id=((me_g + a) % n_grp, (me_s + b) % n_sub), device_id_type=MESH,
        ).start()
    pltpu.make_async_copy(recv2.at[pl.ds(1, n_grp - 1)], recv2.at[pl.ds(1, n_grp - 1)], got2).wait()

    rows_in = jnp.concatenate([recv2[k] for k in range(n_grp)], 0)
    field = matmul(forward_y, rows_in)
    mean = jnp.sum(jnp.where(still, field, 0.0)) * (1.0 / HALF)
    field = jnp.where(still, field - mean, field) * first_scale
    for level in range(6):
        step = 1 << level
        field = (
            scale_r[level] * field
            + scale_p[level] * pltpu.roll(field, step, axis=1)
            + scale_q[level] * pltpu.roll(field, LANES - step, axis=1)
        )
    back = matmul(backward_y, field)[0:4]
    msg3[...] = back
    recv3[0] = back
    for step in sub_steps:
        pltpu.make_async_remote_copy(
            src_ref=msg3, dst_ref=recv3.at[slot(step, sub_size)], send_sem=send3, recv_sem=got3,
            device_id=(me_g, moved(me_s, step, sub_size)), device_id_type=MESH,
        ).start()

    pltpu.make_async_copy(halo, halo, halo_recv).wait()
    big[:, 12:16, :] = jnp.zeros((12, 4, LANES), jnp.float32)
    big[4:8, 4:8, :] = res_ref[...]
    for place, (a, b) in enumerate(ring):
        at_y = {0: 4, 1: 0, n_grp - 1: 8}[a]
        at_x = {0: 4, 1: 0, n_sub - 1: 8}[b]
        big[at_y : at_y + 4, at_x : at_x + 4, :] = halo[place]
    wide = big[...]
    coef1 = tuple(value[:, 0:1] for value in coef8)
    damp1 = damp8[None, 0:1]
    first_w = damp1 * wide
    inner_w = first_w[1:-1] + damp1 * (
        wide[1:-1] - operate(first_w[1:-1], first_w[:-2], first_w[2:], coef1)
    )
    smooth_ref[...] = inner_w[1:-1]
    smooth = smooth_ref[:, 2:10, :]
    near = big[2:10, 2:10, :]

    pltpu.make_async_copy(recv3.at[pl.ds(1, n_sub - 1)], recv3.at[pl.ds(1, n_sub - 1)], got3).wait()
    for j in range(4):
        total = table[j, 0:1, :] * recv3[0]
        for k in range(1, n_sub):
            total = total + table[j, k : k + 1, :] * recv3[k]
        pairs[pl.ds(2 * j, 4, stride=8), :] = total
        pairs[pl.ds(2 * j + 1, 4, stride=8), :] = total
    for j in (1, 2):
        both = pairs[pl.ds(8 * j + 2, 2, stride=2), :]
        coarse_ref[j - 1] = (both + pltpu.roll(both, HALF, axis=1))[:, 0:HALF]
    spread_z = jnp.where((z_out >> 1) == (z_in & (HALF - 1)), 1.0, 0.0)
    coarse = matmul(pairs[...], spread_z)
    lifted = smooth + jnp.concatenate(
        [coarse[8 * (j // 2) : 8 * (j // 2) + 8][None] for j in range(8)], 0
    )
    lifted = lifted[1:-1] + damp8[None] * (
        near[1:-1] - operate(lifted[1:-1], lifted[:-2], lifted[2:], coef8)
    )
    lifted = lifted[1:-1] + damp8[None] * (
        near[2:-2] - operate(lifted[1:-1], lifted[:-2], lifted[2:], coef8)
    )
    cor_ref[...] = lifted[:, 2:6, :]

    pltpu.make_async_copy(halo, halo, halo_send).wait()
    pltpu.make_async_copy(recv1.at[pl.ds(1, n_sub - 1)], recv1.at[pl.ds(1, n_sub - 1)], send1).wait()
    pltpu.make_async_copy(recv2.at[pl.ds(1, n_grp - 1)], recv2.at[pl.ds(1, n_grp - 1)], send2).wait()
    pltpu.make_async_copy(recv3.at[pl.ds(1, n_sub - 1)], recv3.at[pl.ds(1, n_sub - 1)], send3).wait()


def on_device(n_grp, n_sub, residual4, spacing):
    f32 = jnp.float32
    ny5 = 2 * n_grp
    dma = pltpu.SemaphoreType.DMA
    vmem = pl.BlockSpec(memory_space=pltpu.VMEM)
    anywhere = pl.BlockSpec(memory_space=pl.ANY)
    correction, coarse = pl.pallas_call(
        functools.partial(kernel, n_grp, n_sub),
        out_shape=(
            jax.ShapeDtypeStruct((4, 4, LANES), f32),
            jax.ShapeDtypeStruct((2, 2, HALF), f32),
        ),
        in_specs=[anywhere, anywhere],
        out_specs=(vmem, vmem),
        scratch_shapes=[
            pltpu.VMEM((4, 4, LANES), f32),
            pltpu.VMEM((1, LANES), f32),
            pltpu.VMEM((8, 8, LANES), f32),
            pltpu.VMEM((4, n_sub, LANES), f32),
            pltpu.VMEM((n_sub, 4, LANES), f32),
            pltpu.VMEM((n_sub, 4, LANES), f32),
            pltpu.VMEM((4, LANES), f32),
            pltpu.VMEM((n_grp, 4, LANES), f32),
            pltpu.VMEM((4, LANES), f32),
            pltpu.VMEM((n_sub, 4, LANES), f32),
            pltpu.VMEM((8, 4, 4, LANES), f32),
            pltpu.VMEM((12, 16, LANES), f32),
            pltpu.VMEM((8, 16, LANES), f32),
            pltpu.VMEM((32, LANES), f32),
            pltpu.VMEM((6, ny5, LANES), f32),
            pltpu.VMEM((6, ny5, LANES), f32),
            pltpu.VMEM((6, ny5, LANES), f32),
        ]
        + [dma] * 10,
        compiler_params=pltpu.CompilerParams(collective_id=0, has_side_effects=True),
    )(jnp.transpose(residual4, (1, 2, 0)), spacing.reshape(1, LANES))
    return jnp.transpose(correction, (2, 0, 1)), jnp.transpose(coarse, (2, 0, 1))


def solution(mesh):
    placed = P(None, "grp", "sub")
    return jax.shard_map(
        functools.partial(on_device, mesh.shape["grp"], mesh.shape["sub"]),
        mesh=mesh,
        in_specs=(placed, P()),
        out_specs=(placed, placed),
        check_vma=False,
    )
```

```python
import functools
import math

import jax
import jax.numpy as jnp
from jax import lax
from jax.experimental import pallas as pl
from jax.experimental.pallas import tpu as pltpu
from jax.sharding import PartitionSpec as P

MESH = pl.DeviceIdType.MESH
HIGHEST = lax.Precision.HIGHEST
DAMPING = 0.8
LANES = 128
HALF = 64


def matmul(left, right):
    return lax.dot_general(
        left, right, (((1,), (0,)), ((), ())), precision=HIGHEST, preferred_element_type=jnp.float32
    )


def iota(shape, axis):
    return lax.broadcasted_iota(jnp.int32, shape, axis).astype(jnp.float32)


def wrapped(value, count):
    return value - count * jnp.floor((value + 0.5) * (1.0 / count))


def cos_turn(step, count):
    step = jnp.minimum(step, count - step)
    flip = step > count / 4
    step = jnp.where(flip, count / 2 - step, step)
    angle = step * (2.0 * math.pi / count)
    sq = angle * angle
    total = jnp.full_like(sq, 1.0 / math.factorial(16))
    for power in range(14, -1, -2):
        sign = 1.0 if power % 4 == 0 else -1.0
        total = total * sq + sign / math.factorial(power)
    return jnp.where(flip, -total, total)


def up_z(field):
    return pltpu.roll(field, LANES - 1, axis=field.ndim - 1)


def down_z(field):
    return pltpu.roll(field, 1, axis=field.ndim - 1)


def operate(rows, south, north, coef):
    height, upper, lower, diagonal = coef
    span = rows.shape[1]
    west = pltpu.roll(rows, 1, axis=1)
    east = pltpu.roll(rows, span - 1, axis=1)
    sides = (west + east) + (south + north)
    return diagonal * rows - height * sides - upper * up_z(rows) - lower * down_z(rows)


def torus(n_grp, n_sub):
    inner = 8 if n_sub % 8 == 0 else 2
    return (n_grp // 2, 2), (n_sub // inner, inner)


def offsets(sizes):
    outer, inner = sizes

    def hops(step):
        return min(step[0], outer - step[0]) + min(step[1], inner - step[1])

    steps = [(a, b) for a in range(outer) for b in range(inner) if (a, b) != (0, 0)]
    return sorted(steps, key=hops, reverse=True)


def kernel(
    n_grp, n_sub,
    res_hbm, spacing_hbm, cor_ref, coarse_ref,
    res_ref, spacing_ref, pad, table, msg1, recv1, msg2, recv2, msg3, recv3, halo, big, smooth_ref,
    pairs, scale_r, scale_p, scale_q,
    load1, load2, halo_send, halo_recv, send1, got1, send2, got2, send3, got3,
):
    me_g = lax.axis_index("grp")
    me_s = lax.axis_index("sub")
    ny5, nx5 = 2 * n_grp, 2 * n_sub
    grp_size, sub_size = torus(n_grp, n_sub)

    def moved(me, step, sizes):
        outer, inner = sizes
        high, low = me // inner, me % inner
        return ((high + step[0]) % outer) * inner + (low + step[1]) % inner

    def slot(step, sizes):
        outer, inner = sizes
        return (-step[0] % outer) * inner + (-step[1] % inner)

    grp_steps, sub_steps = offsets(grp_size), offsets(sub_size)
    ring = [(a, b) for a in (0, 1, n_grp - 1) for b in (0, 1, n_sub - 1) if (a, b) != (0, 0)]

    load_res = pltpu.make_async_copy(res_hbm, res_ref, load1)
    load_spacing = pltpu.make_async_copy(spacing_hbm, spacing_ref, load2)
    load_res.start()
    load_spacing.start()
    barrier = pltpu.get_barrier_semaphore()

    def greet(device):
        pl.semaphore_signal(barrier, inc=1, device_id=device, device_id_type=MESH)

    for place in range(max(len(grp_steps), len(sub_steps))):
        if place < len(grp_steps):
            greet((moved(me_g, grp_steps[place], grp_size), me_s))
        if place < len(sub_steps):
            greet((me_g, moved(me_s, sub_steps[place], sub_size)))
    for a, b in ring:
        if a and b:
            greet(((me_g + a) % n_grp, (me_s + b) % n_sub))

    shape_t = (n_sub, LANES)
    place_t = lax.broadcasted_iota(jnp.int32, shape_t, 0)
    outer, inner = sub_size
    high = me_s // inner + lax.shift_right_logical(place_t, inner.bit_length() - 1)
    low = me_s % inner + (place_t & (inner - 1))
    high = jnp.where(high >= outer, high - outer, high)
    low = jnp.where(low >= inner, low - inner, low)
    owner = (high * inner + low).astype(jnp.float32)
    second_half = lax.broadcasted_iota(jnp.int32, shape_t, 1) >= HALF
    alone = owner == 0.0
    wave = jnp.where(alone & second_half, 1.0 * n_sub, owner)
    shift = jnp.where(second_half & jnp.logical_not(alone), 0.25 * nx5, 0.0)
    for j in range(4):
        column = wrapped((2 * me_s + (j - 1)).astype(jnp.float32), nx5)
        table[j] = cos_turn(wrapped(wave * column - shift, nx5), nx5)

    load_spacing.wait()
    lane = lax.broadcasted_iota(jnp.int32, (8, LANES), 1)
    height8 = jnp.broadcast_to(spacing_ref[...], (8, LANES))
    face = 2.0 / (height8 + up_z(height8))
    upper8 = jnp.where(lane < LANES - 1, face, 0.0)
    lower8 = jnp.where(lane > 0, down_z(face), 0.0)
    diag8 = 4.0 * height8 + upper8 + lower8
    damp8 = DAMPING / diag8
    coef8 = (height8[None], upper8[None], lower8[None], diag8[None])

    pad[...] = jnp.zeros_like(pad)
    load_res.wait()
    pad[2:6, 2:6, :] = res_ref[...]
    block = pad[...]
    zero_row = jnp.zeros((1, 8, LANES), jnp.float32)

    def operate_zero(rows):
        south = jnp.concatenate([zero_row, rows[:-1]], 0)
        north = jnp.concatenate([rows[1:], zero_row], 0)
        return operate(rows, south, north, coef8)

    first = damp8[None] * block
    second = first + damp8[None] * (block - operate_zero(first))
    leftover = block - operate_zero(second)
    row_pairs = jnp.concatenate([leftover[2 * j] + leftover[2 * j + 1] for j in range(4)], 0)
    z_in = lax.broadcasted_iota(jnp.int32, (LANES, LANES), 0)
    z_out = lax.broadcasted_iota(jnp.int32, (LANES, LANES), 1)
    gather_z = jnp.where((z_in >> 1) == (z_out & (HALF - 1)), 1.0, 0.0)
    pairs[...] = matmul(row_pairs, 0.25 * gather_z)
    parts = [
        pairs[pl.ds(2 * j, 4, stride=8), :] + pairs[pl.ds(2 * j + 1, 4, stride=8), :]
        for j in range(4)
    ]
    for k in range(n_sub):
        total = table[0, k : k + 1, :] * parts[0]
        for j in range(1, 4):
            total = total + table[j, k : k + 1, :] * parts[j]
        if k == 0:
            recv1[0] = total
        else:
            msg1[k] = total

    pl.semaphore_wait(barrier, n_grp + n_sub - 2 + 4)

    for step in sub_steps:
        pltpu.make_async_remote_copy(
            src_ref=msg1.at[step[0] * inner + step[1]], dst_ref=recv1.at[slot(step, sub_size)],
            send_sem=send1, recv_sem=got1,
            device_id=(me_g, moved(me_s, step, sub_size)), device_id_type=MESH,
        ).start()

    lane_m = lax.broadcasted_iota(jnp.int32, (ny5, LANES), 1)
    row_m = lax.broadcasted_iota(jnp.int32, (ny5, LANES), 0)
    z5 = lane_m & (HALF - 1)
    height5 = matmul(height8, gather_z)
    face5 = 2.0 / (height5 + up_z(height5))
    z5_8 = lane & (HALF - 1)
    upper5 = jnp.where(z5_8 < HALF - 1, face5, 0.0)[0:1]
    lower5 = jnp.where(z5_8 > 0, down_z(face5), 0.0)[0:1]
    height5 = height5[0:1]
    mode = row_m.astype(jnp.float32)
    wave_y = jnp.where(mode > n_grp, mode - n_grp, mode)
    sin_y = cos_turn(n_grp - wave_y, 2 * ny5)
    me_sf = me_s.astype(jnp.float32)
    wave_x = jnp.where((lane_m >= HALF) & (me_sf == 0.0), 1.0 * n_sub, me_sf)
    sin_x = cos_turn(n_sub - wave_x, 2 * nx5)
    lam = sin_x * sin_x + sin_y * sin_y
    still = (row_m == 0) & (wave_x == 0.0)
    anchor = jnp.where(still & (z5 == 0), 1.0, 0.0)
    excess = lam * height5 + anchor
    inverse = 1.0 / (excess + upper5 + lower5)
    below = lower5 * inverse
    above = upper5 * inverse
    excess = excess * inverse
    first_scale = inverse
    weight = jnp.where(me_sf == 0.0, 1.0 / nx5, 2.0 / nx5)
    for level in range(6):
        step = 1 << level
        below_dn = pltpu.roll(below, step, axis=1)
        above_up = pltpu.roll(above, LANES - step, axis=1)
        excess_dn = pltpu.roll(excess, step, axis=1)
        excess_up = pltpu.roll(excess, LANES - step, axis=1)
        inverse = 1.0 / (excess + below * (below_dn + excess_dn) + above * (above_up + excess_up))
        low, high = below * inverse, above * inverse
        last = weight if level == 5 else 1.0
        scale_r[level] = inverse * last
        scale_p[level] = low * last
        scale_q[level] = high * last
        excess = excess * inverse + low * excess_dn + high * excess_up
        below, above = low * below_dn, high * above_up

    shape_f = (ny5, 4 * n_grp)
    mode_f, col_f = iota(shape_f, 0), iota(shape_f, 1)
    place_f = jnp.floor((col_f + 0.5) * 0.25)
    pair_f = jnp.floor((place_f + 0.5) * 0.5)
    side = 1.0 - 2.0 * (me_g % 2).astype(jnp.float32)
    row_f = 4.0 * pair_f + 2.0 * side * (place_f - 2.0 * pair_f) + (col_f - 4.0 * place_f) - 1.0
    odd_f = mode_f > n_grp
    phase_f = jnp.where(odd_f, mode_f - n_grp, mode_f) * wrapped(row_f, ny5)
    phase_f = phase_f - jnp.where(odd_f, 0.25 * ny5, 0.0)
    forward_y = cos_turn(wrapped(phase_f, ny5), ny5)
    shape_b = (8, ny5)
    mode_b, row_b = iota(shape_b, 1), iota(shape_b, 0) - 1.0
    odd_b = mode_b > n_grp
    phase_b = jnp.where(odd_b, mode_b - n_grp, mode_b) * row_b - jnp.where(odd_b, 0.25 * ny5, 0.0)
    once = (mode_b == 0.0) | (mode_b == 1.0 * n_grp)
    backward_y = cos_turn(wrapped(phase_b, ny5), ny5) * jnp.where(once, 1.0 / ny5, 2.0 / ny5)

    pltpu.make_async_copy(recv1.at[pl.ds(1, n_sub - 1)], recv1.at[pl.ds(1, n_sub - 1)], got1).wait()
    own = jnp.sum(recv1[...], axis=0)
    msg2[...] = own
    recv2[0] = own
    for step in grp_steps:
        pltpu.make_async_remote_copy(
            src_ref=msg2, dst_ref=recv2.at[slot(step, grp_size)], send_sem=send2, recv_sem=got2,
            device_id=(moved(me_g, step, grp_size), me_s), device_id_type=MESH,
        ).start()
    for place, (a, b) in enumerate(ring):
        pltpu.make_async_remote_copy(
            src_ref=res_ref, dst_ref=halo.at[place], send_sem=halo_send, recv_sem=halo_recv,
            device_id=((me_g + a) % n_grp, (me_s + b) % n_sub), device_id_type=MESH,
        ).start()
    pltpu.make_async_copy(recv2.at[pl.ds(1, n_grp - 1)], recv2.at[pl.ds(1, n_grp - 1)], got2).wait()

    rows_in = jnp.concatenate([recv2[k] for k in range(n_grp)], 0)
    field = matmul(forward_y, rows_in)
    mean = jnp.sum(jnp.where(still, field, 0.0)) * (1.0 / HALF)
    field = jnp.where(still, field - mean, field) * first_scale
    for level in range(6):
        step = 1 << level
        field = (
            scale_r[level] * field
            + scale_p[level] * pltpu.roll(field, step, axis=1)
            + scale_q[level] * pltpu.roll(field, LANES - step, axis=1)
        )
    back = matmul(backward_y, field)[0:4]
    msg3[...] = back
    recv3[0] = back
    for step in sub_steps:
        pltpu.make_async_remote_copy(
            src_ref=msg3, dst_ref=recv3.at[slot(step, sub_size)], send_sem=send3, recv_sem=got3,
            device_id=(me_g, moved(me_s, step, sub_size)), device_id_type=MESH,
        ).start()

    pltpu.make_async_copy(halo, halo, halo_recv).wait()
    big[:, 12:16, :] = jnp.zeros((12, 4, LANES), jnp.float32)
    big[4:8, 4:8, :] = res_ref[...]
    for place, (a, b) in enumerate(ring):
        at_y = {0: 4, 1: 0, n_grp - 1: 8}[a]
        at_x = {0: 4, 1: 0, n_sub - 1: 8}[b]
        big[at_y : at_y + 4, at_x : at_x + 4, :] = halo[place]
    wide = big[...]
    coef1 = tuple(value[:, 0:1] for value in coef8)
    damp1 = damp8[None, 0:1]
    first_w = damp1 * wide
    inner_w = first_w[1:-1] + damp1 * (
        wide[1:-1] - operate(first_w[1:-1], first_w[:-2], first_w[2:], coef1)
    )
    smooth_ref[...] = inner_w[1:-1]
    smooth = smooth_ref[:, 2:10, :]
    near = big[2:10, 2:10, :]

    pltpu.make_async_copy(recv3.at[pl.ds(1, n_sub - 1)], recv3.at[pl.ds(1, n_sub - 1)], got3).wait()
    for j in range(4):
        total = table[j, 0:1, :] * recv3[0]
        for k in range(1, n_sub):
            total = total + table[j, k : k + 1, :] * recv3[k]
        pairs[pl.ds(2 * j, 4, stride=8), :] = total
        pairs[pl.ds(2 * j + 1, 4, stride=8), :] = total
    for j in (1, 2):
        both = pairs[pl.ds(8 * j + 2, 2, stride=2), :]
        coarse_ref[j - 1] = (both + pltpu.roll(both, HALF, axis=1))[:, 0:HALF]
    spread_z = jnp.where((z_out >> 1) == (z_in & (HALF - 1)), 1.0, 0.0)
    coarse = matmul(pairs[...], spread_z)
    lifted = smooth + jnp.concatenate(
        [coarse[8 * (j // 2) : 8 * (j // 2) + 8][None] for j in range(8)], 0
    )
    lifted = lifted[1:-1] + damp8[None] * (
        near[1:-1] - operate(lifted[1:-1], lifted[:-2], lifted[2:], coef8)
    )
    lifted = lifted[1:-1] + damp8[None] * (
        near[2:-2] - operate(lifted[1:-1], lifted[:-2], lifted[2:], coef8)
    )
    cor_ref[...] = lifted[:, 2:6, :]

    pltpu.make_async_copy(halo, halo, halo_send).wait()
    pltpu.make_async_copy(recv1.at[pl.ds(1, n_sub - 1)], recv1.at[pl.ds(1, n_sub - 1)], send1).wait()
    pltpu.make_async_copy(recv2.at[pl.ds(1, n_grp - 1)], recv2.at[pl.ds(1, n_grp - 1)], send2).wait()
    pltpu.make_async_copy(recv3.at[pl.ds(1, n_sub - 1)], recv3.at[pl.ds(1, n_sub - 1)], send3).wait()


def hand_over(cor_in, coarse_in, cor_out, coarse_out, sem1, sem2):
    first = pltpu.make_async_copy(cor_in, cor_out, sem1)
    second = pltpu.make_async_copy(coarse_in, coarse_out, sem2)
    first.start()
    second.start()
    first.wait()
    second.wait()


def on_device(n_grp, n_sub, residual4, spacing):
    f32 = jnp.float32
    ny5 = 2 * n_grp
    dma = pltpu.SemaphoreType.DMA
    vmem = pl.BlockSpec(memory_space=pltpu.VMEM)
    anywhere = pl.BlockSpec(memory_space=pl.ANY)
    correction, coarse = pl.pallas_call(
        functools.partial(kernel, n_grp, n_sub),
        out_shape=(
            pltpu.VMEM((4, 4, LANES), f32),
            pltpu.VMEM((2, 2, HALF), f32),
        ),
        in_specs=[anywhere, anywhere],
        out_specs=(vmem, vmem),
        scratch_shapes=[
            pltpu.VMEM((4, 4, LANES), f32),
            pltpu.VMEM((1, LANES), f32),
            pltpu.VMEM((8, 8, LANES), f32),
            pltpu.VMEM((4, n_sub, LANES), f32),
            pltpu.VMEM((n_sub, 4, LANES), f32),
            pltpu.VMEM((n_sub, 4, LANES), f32),
            pltpu.VMEM((4, LANES), f32),
            pltpu.VMEM((n_grp, 4, LANES), f32),
            pltpu.VMEM((4, LANES), f32),
            pltpu.VMEM((n_sub, 4, LANES), f32),
            pltpu.VMEM((8, 4, 4, LANES), f32),
            pltpu.VMEM((12, 16, LANES), f32),
            pltpu.VMEM((8, 16, LANES), f32),
            pltpu.VMEM((32, LANES), f32),
            pltpu.VMEM((6, ny5, LANES), f32),
            pltpu.VMEM((6, ny5, LANES), f32),
            pltpu.VMEM((6, ny5, LANES), f32),
        ]
        + [dma] * 10,
        compiler_params=pltpu.CompilerParams(collective_id=0, has_side_effects=True),
    )(jnp.transpose(residual4, (1, 2, 0)), spacing.reshape(1, LANES))
    correction, coarse = pl.pallas_call(
        hand_over,
        out_shape=(
            jax.ShapeDtypeStruct((4, 4, LANES), f32),
            jax.ShapeDtypeStruct((2, 2, HALF), f32),
        ),
        in_specs=[vmem, vmem],
        out_specs=(anywhere, anywhere),
        scratch_shapes=[dma] * 2,
    )(
        pltpu.with_memory_space_constraint(correction, pltpu.VMEM),
        pltpu.with_memory_space_constraint(coarse, pltpu.VMEM),
    )
    return jnp.transpose(correction, (2, 0, 1)), jnp.transpose(coarse, (2, 0, 1))


def solution(mesh):
    placed = P(None, "grp", "sub")
    return jax.shard_map(
        functools.partial(on_device, mesh.shape["grp"], mesh.shape["sub"]),
        mesh=mesh,
        in_specs=(placed, P()),
        out_specs=(placed, placed),
        check_vma=False,
    )
```

```python
import functools
import math

import jax
import jax.numpy as jnp
from jax import lax
from jax.experimental import pallas as pl
from jax.experimental.pallas import tpu as pltpu
from jax.sharding import PartitionSpec as P

MESH = pl.DeviceIdType.MESH
HIGHEST = lax.Precision.HIGHEST
DAMPING = 0.8
LANES = 128
HALF = 64
REACH = 7


def matmul(left, right):
    return lax.dot_general(
        left, right, (((1,), (0,)), ((), ())), precision=HIGHEST, preferred_element_type=jnp.float32
    )


def iota(shape, axis):
    return lax.broadcasted_iota(jnp.int32, shape, axis).astype(jnp.float32)


def wrapped(value, count):
    return value - count * jnp.floor((value + 0.5) * (1.0 / count))


def cos_turn(step, count):
    step = jnp.minimum(step, count - step)
    flip = step > count / 4
    step = jnp.where(flip, count / 2 - step, step)
    angle = step * (2.0 * math.pi / count)
    sq = angle * angle
    total = jnp.full_like(sq, 1.0 / math.factorial(16))
    for power in range(14, -1, -2):
        sign = 1.0 if power % 4 == 0 else -1.0
        total = total * sq + sign / math.factorial(power)
    return jnp.where(flip, -total, total)


def up_z(field):
    return pltpu.roll(field, LANES - 1, axis=field.ndim - 1)


def down_z(field):
    return pltpu.roll(field, 1, axis=field.ndim - 1)


def operate(rows, south, north, coef):
    height, upper, lower, diagonal = coef
    span = rows.shape[1]
    west = pltpu.roll(rows, 1, axis=1)
    east = pltpu.roll(rows, span - 1, axis=1)
    sides = (west + east) + (south + north)
    return diagonal * rows - height * sides - upper * up_z(rows) - lower * down_z(rows)


def torus(n_sub):
    inner = 8 if n_sub % 8 == 0 else 2
    return n_sub // inner, inner


def ring_hops(step, size):
    return min(step % size, -step % size)


def hops(step, sizes):
    return ring_hops(step[0], sizes[0]) + ring_hops(step[1], sizes[1])


def compose(weights, keep, down, up, step):
    terms = {}
    for offset, weight in weights.items():
        for place, part in (
            (offset, keep * weight),
            (offset - step, down * pltpu.roll(weight, step, axis=1)),
            (offset + step, up * pltpu.roll(weight, LANES - step, axis=1)),
        ):
            terms[place] = terms[place] + part if place in terms else part
    return terms


def arrived(blocks, semaphore):
    pltpu.make_async_copy(blocks, blocks, semaphore).wait()


def solve_modes(n_grp, n_sub, me_s, height5, weights_z, forward_ref, backward_ref, still_ref):
    ny5, nx5 = 2 * n_grp, 2 * n_sub
    lane_m = lax.broadcasted_iota(jnp.int32, (ny5, LANES), 1)
    row_m = lax.broadcasted_iota(jnp.int32, (ny5, LANES), 0)
    z5 = lane_m & (HALF - 1)
    z5_8 = z5[0:8]
    face5 = 2.0 / (height5 + up_z(height5))
    upper5 = jnp.where(z5_8 < HALF - 1, face5, 0.0)[0:1]
    lower5 = jnp.where(z5_8 > 0, down_z(face5), 0.0)[0:1]
    height5 = height5[0:1]
    mode = row_m.astype(jnp.float32)
    odd = mode > n_grp
    wave_y = jnp.where(odd, mode - n_grp, mode)
    sin_y = cos_turn(n_grp - wave_y, 2 * ny5)
    me_sf = me_s.astype(jnp.float32)
    wave_x = jnp.where((lane_m >= HALF) & (me_sf == 0.0), 1.0 * n_sub, me_sf)
    sin_x = cos_turn(n_sub - wave_x, 2 * nx5)
    lam = sin_x * sin_x + sin_y * sin_y
    still = (row_m == 0) & (wave_x == 0.0)
    still_ref[...] = jnp.where(still, 1.0, 0.0)
    anchor = jnp.where(still & (z5 == 0), 1.0, 0.0)
    excess = lam * height5 + anchor
    inverse = 1.0 / (excess + upper5 + lower5)
    below = lower5 * inverse
    above = upper5 * inverse
    excess = excess * inverse
    weight = jnp.where(me_sf == 0.0, 1.0 / nx5, 2.0 / nx5)
    terms = {0: inverse}
    for level in range(6):
        step = 1 << level
        below_dn = pltpu.roll(below, step, axis=1)
        above_up = pltpu.roll(above, LANES - step, axis=1)
        excess_dn = pltpu.roll(excess, step, axis=1)
        excess_up = pltpu.roll(excess, LANES - step, axis=1)
        inverse = 1.0 / (excess + below * (below_dn + excess_dn) + above * (above_up + excess_up))
        low, high = below * inverse, above * inverse
        last = weight if level == 5 else 1.0
        keep, down, up = inverse * last, low * last, high * last
        terms = (
            {0: keep, -step: down, step: up} if level == 3 else compose(terms, keep, down, up, step)
        )
        if level % 3 == 2:
            for offset in range(-REACH, REACH + 1):
                weights_z[level // 3, REACH + offset] = terms[offset * (step >> 2)]
        excess = excess * inverse + low * excess_dn + high * excess_up
        below, above = low * below_dn, high * above_up

    shape_f = (ny5, 4 * n_grp)
    mode_f, col_f = iota(shape_f, 0), iota(shape_f, 1)
    chip_f = jnp.floor((col_f + 0.5) * 0.125)
    row_f = wrapped(4.0 * chip_f + (col_f - 8.0 * chip_f) - 1.0, ny5)
    odd_f = mode_f > n_grp
    phase_f = jnp.where(odd_f, mode_f - n_grp, mode_f) * row_f - jnp.where(odd_f, 0.25 * ny5, 0.0)
    forward_ref[...] = cos_turn(wrapped(phase_f, ny5), ny5)
    scale = jnp.where((wave_y == 0.0) | (wave_y == 1.0 * n_grp), 1.0 / ny5, 2.0 / ny5)
    quarter = jnp.where(odd, 0.25 * ny5, 0.0)
    for r in range(6):
        backward_ref[r] = cos_turn(wrapped(wave_y * (r - 1.0) - quarter, ny5), ny5) * scale


def kernel(
    n_grp, n_sub,
    res_hbm, spacing_hbm, cor_ref, coarse_ref,
    res_ref, spacing_ref, pad, table, msg1, recv1, msg2, recv2, msg3, recv3, halo, big, smooth_ref,
    pairs, weights_z, forward_ref, backward_ref, still_ref, spread_ref,
    load1, load2, halo_send, halo_recv, send1, got1, send2, got2, send3, got3,
):
    me_g = lax.axis_index("grp")
    me_s = lax.axis_index("sub")
    ny5, nx5 = 2 * n_grp, 2 * n_sub
    n_z = n_grp // 2
    sizes = torus(n_sub)
    outer, inner = sizes
    me_z, side = me_g // 2, me_g % 2
    owner_g, other_g = 2 * me_z + 1, 2 * me_z
    owns = side == 1

    def moved(step):
        return ((me_s // inner + step[0]) % outer) * inner + (me_s % inner + step[1]) % inner

    def slot(step):
        return (-step[0] % outer) * inner + (-step[1] % inner)

    here = [(a, b) for a in range(outer) for b in range(inner)]
    here.sort(key=lambda step: hops(step, sizes), reverse=True)
    away = [step for step in here if step != (0, 0)]
    along_z = sorted(range(1, n_z), key=lambda step: ring_hops(step, n_z), reverse=True)
    ring = [(a, b) for a in (0, 1, n_grp - 1) for b in (0, 1, n_sub - 1) if (a, b) != (0, 0)]

    load_res = pltpu.make_async_copy(res_hbm, res_ref, load1)
    load_spacing = pltpu.make_async_copy(spacing_hbm, spacing_ref, load2)
    load_res.start()
    load_spacing.start()
    barrier = pltpu.get_barrier_semaphore()

    def greet(device):
        pl.semaphore_signal(barrier, inc=1, device_id=device, device_id_type=MESH)

    @pl.when(owns)
    def _():
        queue = [(hops(step, sizes), 0, step) for step in here]
        queue += [(hops(step, sizes), 1, step) for step in away]
        queue += [(ring_hops(step, n_z), 2, step) for step in along_z]
        for _, kind, step in sorted(queue, reverse=True):
            if kind == 2:
                greet((2 * ((me_z + step) % n_z) + 1, me_s))
            else:
                greet((owner_g if kind else other_g, moved(step)))
        for b in (0, 1, n_sub - 1):
            greet(((me_g + 1) % n_grp, (me_s + b) % n_sub))

    @pl.when(jnp.logical_not(owns))
    def _():
        for step in here:
            greet((owner_g, moved(step)))
        for b in (1, n_sub - 1):
            greet((me_g, (me_s + b) % n_sub))
        for b in (0, 1, n_sub - 1):
            greet(((me_g + n_grp - 1) % n_grp, (me_s + b) % n_sub))

    shape_t = (n_sub, LANES)
    place_t = lax.broadcasted_iota(jnp.int32, shape_t, 0)
    high = me_s // inner + lax.shift_right_logical(place_t, inner.bit_length() - 1)
    low = me_s % inner + (place_t & (inner - 1))
    high = jnp.where(high >= outer, high - outer, high)
    low = jnp.where(low >= inner, low - inner, low)
    owner = (high * inner + low).astype(jnp.float32)
    second_half = lax.broadcasted_iota(jnp.int32, shape_t, 1) >= HALF
    alone = owner == 0.0
    wave = jnp.where(alone & second_half, 1.0 * n_sub, owner)
    shift = jnp.where(second_half & jnp.logical_not(alone), 0.25 * nx5, 0.0)
    for j in range(4):
        column = wrapped((2 * me_s + (j - 1)).astype(jnp.float32), nx5)
        table[j] = cos_turn(wrapped(wave * column - shift, nx5), nx5)

    load_spacing.wait()
    lane = lax.broadcasted_iota(jnp.int32, (8, LANES), 1)
    height8 = jnp.broadcast_to(spacing_ref[...], (8, LANES))
    face = 2.0 / (height8 + up_z(height8))
    upper8 = jnp.where(lane < LANES - 1, face, 0.0)
    lower8 = jnp.where(lane > 0, down_z(face), 0.0)
    diag8 = 4.0 * height8 + upper8 + lower8
    damp8 = DAMPING / diag8
    coef8 = (height8[None], upper8[None], lower8[None], diag8[None])

    pad[...] = jnp.zeros_like(pad)
    load_res.wait()
    pad[2:6, 2:6, :] = res_ref[...]
    block = pad[...]
    zero_row = jnp.zeros((1, 8, LANES), jnp.float32)

    def operate_zero(rows):
        south = jnp.concatenate([zero_row, rows[:-1]], 0)
        north = jnp.concatenate([rows[1:], zero_row], 0)
        return operate(rows, south, north, coef8)

    first = damp8[None] * block
    second = first + damp8[None] * (block - operate_zero(first))
    leftover = block - operate_zero(second)
    row_pairs = jnp.concatenate([leftover[2 * j] + leftover[2 * j + 1] for j in range(4)], 0)
    z_in = lax.broadcasted_iota(jnp.int32, (LANES, LANES), 0)
    z_out = lax.broadcasted_iota(jnp.int32, (LANES, LANES), 1)
    gather_z = jnp.where((z_in >> 1) == (z_out & (HALF - 1)), 1.0, 0.0)
    pairs[...] = matmul(row_pairs, 0.25 * gather_z)
    parts = [
        pairs[pl.ds(2 * j, 4, stride=8), :] + pairs[pl.ds(2 * j + 1, 4, stride=8), :]
        for j in range(4)
    ]
    for k in range(n_sub):
        total = table[0, k : k + 1, :] * parts[0]
        for j in range(1, 4):
            total = total + table[j, k : k + 1, :] * parts[j]
        msg1[k] = total

    spread_ref[...] = jnp.where((z_out >> 1) == (z_in & (HALF - 1)), 1.0, 0.0)

    pl.semaphore_wait(barrier, jnp.where(owns, 2 * n_sub - 1 + n_z - 1 + 3, n_sub + 5))

    for step in away:
        pltpu.make_async_remote_copy(
            src_ref=msg1.at[step[0] * inner + step[1]],
            dst_ref=recv1.at[side * n_sub + slot(step)], send_sem=send1, recv_sem=got1,
            device_id=(owner_g, moved(step)), device_id_type=MESH,
        ).start()

    @pl.when(jnp.logical_not(owns))
    def _():
        pltpu.make_async_remote_copy(
            src_ref=msg1.at[0], dst_ref=recv1.at[0], send_sem=send1, recv_sem=got1,
            device_id=(owner_g, me_s), device_id_type=MESH,
        ).start()

    for place, (a, b) in enumerate(ring):
        pltpu.make_async_remote_copy(
            src_ref=res_ref, dst_ref=halo.at[place], send_sem=halo_send, recv_sem=halo_recv,
            device_id=((me_g + a) % n_grp, (me_s + b) % n_sub), device_id_type=MESH,
        ).start()

    height5 = matmul(height8, gather_z)

    @pl.when(owns)
    def _():
        recv1[n_sub] = msg1[0]
        solve_modes(
            n_grp, n_sub, me_s, height5, weights_z, forward_ref, backward_ref, still_ref
        )
        arrived(recv1.at[pl.ds(0, 2 * n_sub - 1)], got1)
        other = jnp.sum(recv1[0:n_sub], axis=0)
        own = jnp.sum(recv1[n_sub : 2 * n_sub], axis=0)
        gap = jnp.zeros((2, LANES), jnp.float32)
        both = jnp.concatenate([other, gap, gap], 0) + jnp.concatenate([gap, own, gap], 0)
        msg2[...] = both
        recv2[0] = both
        for step in along_z:
            pltpu.make_async_remote_copy(
                src_ref=msg2, dst_ref=recv2.at[-step % n_z], send_sem=send2, recv_sem=got2,
                device_id=(2 * ((me_z + step) % n_z) + 1, me_s), device_id_type=MESH,
            ).start()
        arrived(recv2.at[pl.ds(1, n_z - 1)], got2)

        rows_in = recv2[...].reshape(8 * n_z, LANES)
        field = matmul(forward_ref[...], rows_in)
        column = jnp.sum(rows_in, axis=0, keepdims=True)
        low_half = lax.broadcasted_iota(jnp.int32, (1, LANES), 1) < HALF
        mean = jnp.sum(jnp.where(low_half, column, 0.0), axis=1, keepdims=True) * (1.0 / HALF)
        field = field - still_ref[...] * mean
        for group in range(2):
            total = weights_z[group, REACH] * field
            for offset in range(1, REACH + 1):
                step = offset << (3 * group)
                total = total + (
                    weights_z[group, REACH - offset] * pltpu.roll(field, step, axis=1)
                    + weights_z[group, REACH + offset] * pltpu.roll(field, LANES - step, axis=1)
                )
            field = total
        lines = []
        for r in range(6):
            line = backward_ref[r, 0:8] * field[0:8]
            for k in range(8, ny5, 8):
                line = line + backward_ref[r, k : k + 8] * field[k : k + 8]
            lines.append(jnp.sum(line, axis=0, keepdims=True))
        msg3[0] = jnp.concatenate(lines[0:4], 0)
        msg3[1] = jnp.concatenate(lines[2:6], 0)
        recv3[0] = msg3[1]
        for step in here:
            for core in (0, 1):
                if core == 0 or step != (0, 0):
                    pltpu.make_async_remote_copy(
                        src_ref=msg3.at[core], dst_ref=recv3.at[slot(step)],
                        send_sem=send3, recv_sem=got3,
                        device_id=(owner_g if core else other_g, moved(step)),
                        device_id_type=MESH,
                    ).start()

    arrived(halo, halo_recv)
    big[:, 12:16, :] = jnp.zeros((12, 4, LANES), jnp.float32)
    big[4:8, 4:8, :] = res_ref[...]
    for place, (a, b) in enumerate(ring):
        at_y = {0: 4, 1: 0, n_grp - 1: 8}[a]
        at_x = {0: 4, 1: 0, n_sub - 1: 8}[b]
        big[at_y : at_y + 4, at_x : at_x + 4, :] = halo[place]
    wide = big[...]
    coef1 = tuple(value[:, 0:1] for value in coef8)
    damp1 = damp8[None, 0:1]
    first_w = damp1 * wide
    inner_w = first_w[1:-1] + damp1 * (
        wide[1:-1] - operate(first_w[1:-1], first_w[:-2], first_w[2:], coef1)
    )
    smooth_ref[...] = inner_w[1:-1]
    smooth = smooth_ref[:, 2:10, :]
    near = big[2:10, 2:10, :]

    @pl.when(owns)
    def _():
        arrived(recv3.at[pl.ds(1, n_sub - 1)], got3)

    @pl.when(jnp.logical_not(owns))
    def _():
        arrived(recv3, got3)

    for j in range(4):
        total = table[j, 0:1, :] * recv3[0]
        for k in range(1, n_sub):
            total = total + table[j, k : k + 1, :] * recv3[k]
        pairs[pl.ds(2 * j, 4, stride=8), :] = total
        pairs[pl.ds(2 * j + 1, 4, stride=8), :] = total
    for j in (1, 2):
        both = pairs[pl.ds(8 * j + 2, 2, stride=2), :]
        coarse_ref[j - 1] = (both + pltpu.roll(both, HALF, axis=1))[:, 0:HALF]
    coarse = matmul(pairs[...], spread_ref[...])
    lifted = smooth + jnp.concatenate(
        [coarse[8 * (j // 2) : 8 * (j // 2) + 8][None] for j in range(8)], 0
    )
    lifted = lifted[1:-1] + damp8[None] * (
        near[1:-1] - operate(lifted[1:-1], lifted[:-2], lifted[2:], coef8)
    )
    lifted = lifted[1:-1] + damp8[None] * (
        near[2:-2] - operate(lifted[1:-1], lifted[:-2], lifted[2:], coef8)
    )
    cor_ref[...] = lifted[:, 2:6, :]

    arrived(halo, halo_send)

    @pl.when(owns)
    def _():
        arrived(recv1.at[pl.ds(0, n_sub - 1)], send1)
        arrived(recv2.at[pl.ds(1, n_z - 1)], send2)
        arrived(recv1.at[pl.ds(0, 2 * n_sub - 1)], send3)

    @pl.when(jnp.logical_not(owns))
    def _():
        arrived(recv1.at[pl.ds(0, n_sub)], send1)


def hand_over(cor_in, coarse_in, cor_out, coarse_out, sem1, sem2):
    first = pltpu.make_async_copy(cor_in, cor_out, sem1)
    second = pltpu.make_async_copy(coarse_in, coarse_out, sem2)
    first.start()
    second.start()
    first.wait()
    second.wait()


def on_device(n_grp, n_sub, residual4, spacing):
    f32 = jnp.float32
    ny5 = 2 * n_grp
    dma = pltpu.SemaphoreType.DMA
    vmem = pl.BlockSpec(memory_space=pltpu.VMEM)
    anywhere = pl.BlockSpec(memory_space=pl.ANY)
    correction, coarse = pl.pallas_call(
        functools.partial(kernel, n_grp, n_sub),
        out_shape=(
            pltpu.VMEM((4, 4, LANES), f32),
            pltpu.VMEM((2, 2, HALF), f32),
        ),
        in_specs=[anywhere, anywhere],
        out_specs=(vmem, vmem),
        scratch_shapes=[
            pltpu.VMEM((4, 4, LANES), f32),
            pltpu.VMEM((1, LANES), f32),
            pltpu.VMEM((8, 8, LANES), f32),
            pltpu.VMEM((4, n_sub, LANES), f32),
            pltpu.VMEM((n_sub, 4, LANES), f32),
            pltpu.VMEM((2 * n_sub, 4, LANES), f32),
            pltpu.VMEM((8, LANES), f32),
            pltpu.VMEM((n_grp // 2, 8, LANES), f32),
            pltpu.VMEM((2, 4, LANES), f32),
            pltpu.VMEM((n_sub, 4, LANES), f32),
            pltpu.VMEM((8, 4, 4, LANES), f32),
            pltpu.VMEM((12, 16, LANES), f32),
            pltpu.VMEM((8, 16, LANES), f32),
            pltpu.VMEM((32, LANES), f32),
            pltpu.VMEM((2, 2 * REACH + 1, ny5, LANES), f32),
            pltpu.VMEM((ny5, 4 * n_grp), f32),
            pltpu.VMEM((6, ny5, LANES), f32),
            pltpu.VMEM((ny5, LANES), f32),
            pltpu.VMEM((LANES, LANES), f32),
        ]
        + [dma] * 10,
        compiler_params=pltpu.CompilerParams(collective_id=0, has_side_effects=True),
    )(jnp.transpose(residual4, (1, 2, 0)), spacing.reshape(1, LANES))
    correction, coarse = pl.pallas_call(
        hand_over,
        out_shape=(
            jax.ShapeDtypeStruct((4, 4, LANES), f32),
            jax.ShapeDtypeStruct((2, 2, HALF), f32),
        ),
        in_specs=[vmem, vmem],
        out_specs=(anywhere, anywhere),
        scratch_shapes=[dma] * 2,
    )(
        pltpu.with_memory_space_constraint(correction, pltpu.VMEM),
        pltpu.with_memory_space_constraint(coarse, pltpu.VMEM),
    )
    return jnp.transpose(correction, (2, 0, 1)), jnp.transpose(coarse, (2, 0, 1))


def solution(mesh):
    placed = P(None, "grp", "sub")
    return jax.shard_map(
        functools.partial(on_device, mesh.shape["grp"], mesh.shape["sub"]),
        mesh=mesh,
        in_specs=(placed, P()),
        out_specs=(placed, placed),
        check_vma=False,
    )
```

```python
import functools
import math

import jax
import jax.numpy as jnp
from jax import lax
from jax.experimental import pallas as pl
from jax.experimental.pallas import tpu as pltpu
from jax.sharding import PartitionSpec as P

MESH = pl.DeviceIdType.MESH
HIGHEST = lax.Precision.HIGHEST
DAMPING = 0.8
LANES = 128
HALF = 64
REACH = 7


def matmul(left, right):
    return lax.dot_general(
        left, right, (((1,), (0,)), ((), ())), precision=HIGHEST, preferred_element_type=jnp.float32
    )


def iota(shape, axis):
    return lax.broadcasted_iota(jnp.int32, shape, axis).astype(jnp.float32)


def wrapped(value, count):
    return value - count * jnp.floor((value + 0.5) * (1.0 / count))


def cos_turn(step, count):
    step = jnp.minimum(step, count - step)
    flip = step > count / 4
    step = jnp.where(flip, count / 2 - step, step)
    angle = step * (2.0 * math.pi / count)
    sq = angle * angle
    total = jnp.full_like(sq, 1.0 / math.factorial(16))
    for power in range(14, -1, -2):
        sign = 1.0 if power % 4 == 0 else -1.0
        total = total * sq + sign / math.factorial(power)
    return jnp.where(flip, -total, total)


def up_z(field):
    return pltpu.roll(field, LANES - 1, axis=field.ndim - 1)


def down_z(field):
    return pltpu.roll(field, 1, axis=field.ndim - 1)


def operate(rows, south, north, coef):
    height, upper, lower, diagonal = coef
    span = rows.shape[1]
    west = pltpu.roll(rows, 1, axis=1)
    east = pltpu.roll(rows, span - 1, axis=1)
    sides = (west + east) + (south + north)
    return diagonal * rows - height * sides - upper * up_z(rows) - lower * down_z(rows)


def torus(n_sub):
    inner = 8 if n_sub % 8 == 0 else 2
    return n_sub // inner, inner


def ring_hops(step, size):
    return min(step % size, -step % size)


def hops(step, sizes):
    return ring_hops(step[0], sizes[0]) + ring_hops(step[1], sizes[1])


def compose(weights, keep, down, up, step):
    terms = {}
    for offset, weight in weights.items():
        for place, part in (
            (offset, keep * weight),
            (offset - step, down * pltpu.roll(weight, step, axis=1)),
            (offset + step, up * pltpu.roll(weight, LANES - step, axis=1)),
        ):
            terms[place] = terms[place] + part if place in terms else part
    return terms


def owner_places(n_sub):
    outer, inner = torus(n_sub)

    def rank(place):
        step = (place // inner, place % inner)
        return hops(step, (outer, inner)), step[1]

    return sorted(range(n_sub), key=rank)[: n_sub // 2]


def arrived(blocks, semaphore):
    pltpu.make_async_copy(blocks, blocks, semaphore).wait()


def solve_modes(n_grp, n_sub, wave_f, height5, weights_z, still_ref):
    ny5, nx5 = 2 * n_grp, 2 * n_sub
    lane_m = lax.broadcasted_iota(jnp.int32, (ny5, LANES), 1)
    row_m = lax.broadcasted_iota(jnp.int32, (ny5, LANES), 0)
    z5 = lane_m & (HALF - 1)
    z5_8 = z5[0:8]
    face5 = 2.0 / (height5 + up_z(height5))
    upper5 = jnp.where(z5_8 < HALF - 1, face5, 0.0)[0:1]
    lower5 = jnp.where(z5_8 > 0, down_z(face5), 0.0)[0:1]
    height5 = height5[0:1]
    mode = row_m.astype(jnp.float32)
    odd = mode > n_grp
    wave_y = jnp.where(odd, mode - n_grp, mode)
    sin_y = cos_turn(n_grp - wave_y, 2 * ny5)
    wave_x = jnp.where((lane_m >= HALF) & (wave_f == 0.0), 1.0 * n_sub, wave_f)
    sin_x = cos_turn(n_sub - wave_x, 2 * nx5)
    lam = sin_x * sin_x + sin_y * sin_y
    still = (row_m == 0) & (wave_x == 0.0)
    still_ref[...] = jnp.where(still, 1.0, 0.0)
    anchor = jnp.where(still & (z5 == 0), 1.0, 0.0)
    excess = lam * height5 + anchor
    inverse = 1.0 / (excess + upper5 + lower5)
    below = lower5 * inverse
    above = upper5 * inverse
    excess = excess * inverse
    weight = jnp.where(wave_f == 0.0, 1.0 / nx5, 2.0 / nx5)
    terms = {0: inverse}
    for level in range(6):
        step = 1 << level
        below_dn = pltpu.roll(below, step, axis=1)
        above_up = pltpu.roll(above, LANES - step, axis=1)
        excess_dn = pltpu.roll(excess, step, axis=1)
        excess_up = pltpu.roll(excess, LANES - step, axis=1)
        inverse = 1.0 / (excess + below * (below_dn + excess_dn) + above * (above_up + excess_up))
        low, high = below * inverse, above * inverse
        last = weight if level == 5 else 1.0
        keep, down, up = inverse * last, low * last, high * last
        terms = (
            {0: keep, -step: down, step: up} if level == 3 else compose(terms, keep, down, up, step)
        )
        if level % 3 == 2:
            for offset in range(-REACH, REACH + 1):
                weights_z[level // 3, REACH + offset] = terms[offset * (step >> 2)]
        excess = excess * inverse + low * excess_dn + high * excess_up
        below, above = low * below_dn, high * above_up


def transforms(n_grp, forward_ref, backward_ref):
    ny5 = 2 * n_grp
    mode = iota((ny5, LANES), 0)
    odd = mode > n_grp
    wave_y = jnp.where(odd, mode - n_grp, mode)
    shape_f = (ny5, 4 * n_grp)
    mode_f, col_f = iota(shape_f, 0), iota(shape_f, 1)
    chip_f = jnp.floor((col_f + 0.5) * 0.125)
    row_f = wrapped(4.0 * chip_f + (col_f - 8.0 * chip_f) - 1.0, ny5)
    odd_f = mode_f > n_grp
    phase_f = jnp.where(odd_f, mode_f - n_grp, mode_f) * row_f - jnp.where(odd_f, 0.25 * ny5, 0.0)
    forward_ref[...] = cos_turn(wrapped(phase_f, ny5), ny5)
    scale = jnp.where((wave_y == 0.0) | (wave_y == 1.0 * n_grp), 1.0 / ny5, 2.0 / ny5)
    quarter = jnp.where(odd, 0.25 * ny5, 0.0)
    for r in range(6):
        backward_ref[r] = cos_turn(wrapped(wave_y * (r - 1.0) - quarter, ny5), ny5) * scale


def kernel(
    n_grp, n_sub,
    res_hbm, spacing_hbm, cor_ref, coarse_ref,
    res_ref, spacing_ref, pad, table, table8, msg1, recv1, msg2, recv2, msg3, recv3, halo, big, smooth_ref,
    pairs, weights_z, forward_ref, backward_ref, still_ref, spread_ref,
    load1, load2, halo_send, halo_recv, send1, got1, send2, got2, send3, got3,
):
    me_g = lax.axis_index("grp")
    me_s = lax.axis_index("sub")
    ny5, nx5 = 2 * n_grp, 2 * n_sub
    n_z = n_grp // 2
    sizes = torus(n_sub)
    outer, inner = sizes
    me_z, side = me_g // 2, me_g % 2
    owner_g, other_g = 2 * me_z + 1, 2 * me_z

    def moved(step):
        return ((me_s // inner + step[0]) % outer) * inner + (me_s % inner + step[1]) % inner

    places = owner_places(n_sub)
    n_own = len(places)
    own_index = sum(jnp.where(me_s == place, number, 0) for number, place in enumerate(places))
    chosen = sum(jnp.where(me_s == place, 1, 0) for place in places)
    owns = side * chosen == 1

    here = [(a, b) for a in range(outer) for b in range(inner)]
    here.sort(key=lambda step: hops(step, sizes), reverse=True)
    along_z = sorted(range(1, n_z), key=lambda step: ring_hops(step, n_z), reverse=True)
    ring = [(a, b) for a in (0, 1, n_grp - 1) for b in (0, 1, n_sub - 1) if (a, b) != (0, 0)]

    load_res = pltpu.make_async_copy(res_hbm, res_ref, load1)
    load_spacing = pltpu.make_async_copy(spacing_hbm, spacing_ref, load2)
    load_res.start()
    load_spacing.start()
    barrier = pltpu.get_barrier_semaphore()

    def greet(device):
        pl.semaphore_signal(barrier, inc=1, device_id=device, device_id_type=MESH)

    @pl.when(owns)
    def _():
        queue = [(hops(step, sizes), 0, step) for step in here]
        queue += [(hops(step, sizes), 1, step) for step in here if step != (0, 0)]
        queue += [(ring_hops(step, n_z), 2, step) for step in along_z]
        for _, kind, step in sorted(queue, reverse=True):
            if kind == 2:
                greet((2 * ((me_z + step) % n_z) + 1, me_s))
            else:
                greet((owner_g if kind else other_g, moved(step)))

    @pl.when(jnp.logical_not(owns))
    def _():
        for place in places:
            greet((owner_g, place))

    for a, b in ring:
        greet(((me_g + a) % n_grp, (me_s + b) % n_sub))

    shape_t = (n_sub, LANES)
    owner = iota(shape_t, 0)
    second_half = lax.broadcasted_iota(jnp.int32, shape_t, 1) >= HALF
    alone = owner == 0.0
    wave = jnp.where(alone & second_half, 1.0 * n_sub, owner)
    shift = jnp.where(second_half & jnp.logical_not(alone), 0.25 * nx5, 0.0)
    for j in range(4):
        column = wrapped((2 * me_s + (j - 1)).astype(jnp.float32), nx5)
        table[j] = cos_turn(wrapped(wave * column - shift, nx5), nx5)

    load_spacing.wait()
    lane = lax.broadcasted_iota(jnp.int32, (8, LANES), 1)
    height8 = jnp.broadcast_to(spacing_ref[...], (8, LANES))
    face = 2.0 / (height8 + up_z(height8))
    upper8 = jnp.where(lane < LANES - 1, face, 0.0)
    lower8 = jnp.where(lane > 0, down_z(face), 0.0)
    diag8 = 4.0 * height8 + upper8 + lower8
    damp8 = DAMPING / diag8
    coef8 = (height8[None], upper8[None], lower8[None], diag8[None])

    pad[...] = jnp.zeros_like(pad)
    load_res.wait()
    pad[2:6, 2:6, :] = res_ref[...]
    block = pad[...]
    zero_row = jnp.zeros((1, 8, LANES), jnp.float32)

    def operate_zero(rows):
        south = jnp.concatenate([zero_row, rows[:-1]], 0)
        north = jnp.concatenate([rows[1:], zero_row], 0)
        return operate(rows, south, north, coef8)

    first = damp8[None] * block
    second = first + damp8[None] * (block - operate_zero(first))
    leftover = block - operate_zero(second)
    row_pairs = jnp.concatenate([leftover[2 * j] + leftover[2 * j + 1] for j in range(4)], 0)
    z_in = lax.broadcasted_iota(jnp.int32, (LANES, LANES), 0)
    z_out = lax.broadcasted_iota(jnp.int32, (LANES, LANES), 1)
    gather_z = jnp.where((z_in >> 1) == (z_out & (HALF - 1)), 1.0, 0.0)
    pairs[...] = matmul(row_pairs, 0.25 * gather_z)
    parts = [
        pairs[pl.ds(2 * j, 4, stride=8), :] + pairs[pl.ds(2 * j + 1, 4, stride=8), :]
        for j in range(4)
    ]
    for k in range(n_sub):
        total = table[0, k : k + 1, :] * parts[0]
        for j in range(1, 4):
            total = total + table[j, k : k + 1, :] * parts[j]
        msg1[k // 2, 4 * (k % 2) : 4 * (k % 2) + 4, :] = total

    spread_ref[...] = jnp.where((z_out >> 1) == (z_in & (HALF - 1)), 1.0, 0.0)

    pl.semaphore_wait(barrier, 8 + jnp.where(owns, 2 * n_sub - 1 + n_z - 1, n_own))

    def share(number, place):
        pltpu.make_async_remote_copy(
            src_ref=msg1.at[number], dst_ref=recv1.at[side * n_sub + me_s],
            send_sem=send1, recv_sem=got1,
            device_id=(owner_g, place), device_id_type=MESH,
        ).start()

    for number, place in enumerate(places):
        pl.when(jnp.logical_not(owns) | (me_s != place))(functools.partial(share, number, place))

    for place, (a, b) in enumerate(ring):
        pltpu.make_async_remote_copy(
            src_ref=res_ref, dst_ref=halo.at[place], send_sem=halo_send, recv_sem=halo_recv,
            device_id=((me_g + a) % n_grp, (me_s + b) % n_sub), device_id_type=MESH,
        ).start()

    height5 = matmul(height8, gather_z)

    @pl.when(owns)
    def _():
        recv1[n_sub + me_s] = msg1[own_index]
        transforms(n_grp, forward_ref, backward_ref)
        for pair in range(2):
            wave_f = (2 * own_index + pair).astype(jnp.float32)
            solve_modes(
                n_grp, n_sub, wave_f, height5, weights_z.at[pair], still_ref.at[pair]
            )
        arrived(recv1.at[pl.ds(0, 2 * n_sub - 1)], got1)
        other = jnp.sum(recv1[0:n_sub], axis=0)
        own = jnp.sum(recv1[n_sub : 2 * n_sub], axis=0)
        gap = jnp.zeros((2, LANES), jnp.float32)
        for pair in range(2):
            left, right = other[4 * pair : 4 * pair + 4], own[4 * pair : 4 * pair + 4]
            both = jnp.concatenate([left, gap, gap], 0) + jnp.concatenate([gap, right, gap], 0)
            msg2[pair] = both
            recv2[0, pair] = both
        for step in along_z:
            pltpu.make_async_remote_copy(
                src_ref=msg2, dst_ref=recv2.at[-step % n_z], send_sem=send2, recv_sem=got2,
                device_id=(2 * ((me_z + step) % n_z) + 1, me_s), device_id_type=MESH,
            ).start()
        arrived(recv2.at[pl.ds(1, n_z - 1)], got2)

        fields, means = [], []
        low_half = lax.broadcasted_iota(jnp.int32, (1, LANES), 1) < HALF
        for pair in range(2):
            rows_in = jnp.concatenate([recv2[k, pair] for k in range(n_z)], 0)
            fields.append(matmul(forward_ref[...], rows_in))
            column = jnp.where(low_half, jnp.sum(rows_in, axis=0, keepdims=True), 0.0)
            means.append(jnp.sum(column, axis=1, keepdims=True) * (1.0 / HALF))
        lines = [[], []]
        for pair in range(2):
            field = fields[pair] - still_ref[pair] * means[pair]
            for group in range(2):
                total = weights_z[pair, group, REACH] * field
                for offset in range(1, REACH + 1):
                    step = offset << (3 * group)
                    total = total + (
                        weights_z[pair, group, REACH - offset] * pltpu.roll(field, step, axis=1)
                        + weights_z[pair, group, REACH + offset]
                        * pltpu.roll(field, LANES - step, axis=1)
                    )
                field = total
            for r in range(6):
                line = backward_ref[r, 0:8] * field[0:8]
                for k in range(8, ny5, 8):
                    line = line + backward_ref[r, k : k + 8] * field[k : k + 8]
                lines[pair].append(jnp.sum(line, axis=0, keepdims=True))
        for core, first in ((0, 0), (1, 2)):
            msg3[core] = jnp.concatenate(
                lines[0][first : first + 4] + lines[1][first : first + 4], 0
            )
        recv3[own_index] = msg3[1]

        def give(core, place):
            pltpu.make_async_remote_copy(
                src_ref=msg3.at[core], dst_ref=recv3.at[own_index],
                send_sem=send3, recv_sem=got3,
                device_id=(owner_g if core else other_g, place), device_id_type=MESH,
            ).start()

        in_order = sorted(range(n_sub), key=lambda p: hops((p // inner, p % inner), sizes))
        for place in in_order:
            pl.when(me_s != place)(functools.partial(give, 1, place))
            give(0, place)

    for j in range(4):
        for number in range(n_own):
            table8[j, number] = jnp.concatenate(
                [
                    jnp.broadcast_to(table[j, k : k + 1, :], (4, LANES))
                    for k in (2 * number, 2 * number + 1)
                ],
                0,
            )

    arrived(halo, halo_recv)
    big[:, 12:16, :] = jnp.zeros((12, 4, LANES), jnp.float32)
    big[4:8, 4:8, :] = res_ref[...]
    for place, (a, b) in enumerate(ring):
        at_y = {0: 4, 1: 0, n_grp - 1: 8}[a]
        at_x = {0: 4, 1: 0, n_sub - 1: 8}[b]
        big[at_y : at_y + 4, at_x : at_x + 4, :] = halo[place]
    wide = big[...]
    coef1 = tuple(value[:, 0:1] for value in coef8)
    damp1 = damp8[None, 0:1]
    first_w = damp1 * wide
    inner_w = first_w[1:-1] + damp1 * (
        wide[1:-1] - operate(first_w[1:-1], first_w[:-2], first_w[2:], coef1)
    )
    smooth_ref[...] = inner_w[1:-1]
    smooth = smooth_ref[:, 2:10, :]
    near = big[2:10, 2:10, :]

    @pl.when(owns)
    def _():
        arrived(recv3.at[pl.ds(0, n_own - 1)], got3)

    @pl.when(jnp.logical_not(owns))
    def _():
        arrived(recv3, got3)

    for j in range(4):
        total = table8[j, 0] * recv3[0]
        for k in range(1, n_own):
            total = total + table8[j, k] * recv3[k]
        total = total[0:4] + total[4:8]
        pairs[pl.ds(2 * j, 4, stride=8), :] = total
        pairs[pl.ds(2 * j + 1, 4, stride=8), :] = total
    for j in (1, 2):
        both = pairs[pl.ds(8 * j + 2, 2, stride=2), :]
        coarse_ref[j - 1] = (both + pltpu.roll(both, HALF, axis=1))[:, 0:HALF]
    coarse = matmul(pairs[...], spread_ref[...])
    lifted = smooth + jnp.concatenate(
        [coarse[8 * (j // 2) : 8 * (j // 2) + 8][None] for j in range(8)], 0
    )
    lifted = lifted[1:-1] + damp8[None] * (
        near[1:-1] - operate(lifted[1:-1], lifted[:-2], lifted[2:], coef8)
    )
    lifted = lifted[1:-1] + damp8[None] * (
        near[2:-2] - operate(lifted[1:-1], lifted[:-2], lifted[2:], coef8)
    )
    cor_ref[...] = lifted[:, 2:6, :]

    arrived(halo, halo_send)

    @pl.when(owns)
    def _():
        arrived(recv1.at[pl.ds(0, n_own - 1)], send1)
        arrived(recv2.at[pl.ds(1, n_z - 1)], send2)
        arrived(recv1.at[pl.ds(0, 2 * n_sub - 1)], send3)

    @pl.when(jnp.logical_not(owns))
    def _():
        arrived(recv1.at[pl.ds(0, n_own)], send1)


def hand_over(cor_in, coarse_in, cor_out, coarse_out, sem1, sem2):
    first = pltpu.make_async_copy(cor_in, cor_out, sem1)
    second = pltpu.make_async_copy(coarse_in, coarse_out, sem2)
    first.start()
    second.start()
    first.wait()
    second.wait()


def on_device(n_grp, n_sub, residual4, spacing):
    f32 = jnp.float32
    ny5 = 2 * n_grp
    dma = pltpu.SemaphoreType.DMA
    vmem = pl.BlockSpec(memory_space=pltpu.VMEM)
    anywhere = pl.BlockSpec(memory_space=pl.ANY)
    correction, coarse = pl.pallas_call(
        functools.partial(kernel, n_grp, n_sub),
        out_shape=(
            pltpu.VMEM((4, 4, LANES), f32),
            pltpu.VMEM((2, 2, HALF), f32),
        ),
        in_specs=[anywhere, anywhere],
        out_specs=(vmem, vmem),
        scratch_shapes=[
            pltpu.VMEM((4, 4, LANES), f32),
            pltpu.VMEM((1, LANES), f32),
            pltpu.VMEM((8, 8, LANES), f32),
            pltpu.VMEM((4, n_sub, LANES), f32),
            pltpu.VMEM((4, n_sub // 2, 8, LANES), f32),
            pltpu.VMEM((n_sub // 2, 8, LANES), f32),
            pltpu.VMEM((2 * n_sub, 8, LANES), f32),
            pltpu.VMEM((2, 8, LANES), f32),
            pltpu.VMEM((n_grp // 2, 2, 8, LANES), f32),
            pltpu.VMEM((2, 8, LANES), f32),
            pltpu.VMEM((n_sub // 2, 8, LANES), f32),
            pltpu.VMEM((8, 4, 4, LANES), f32),
            pltpu.VMEM((12, 16, LANES), f32),
            pltpu.VMEM((8, 16, LANES), f32),
            pltpu.VMEM((32, LANES), f32),
            pltpu.VMEM((2, 2, 2 * REACH + 1, ny5, LANES), f32),
            pltpu.VMEM((ny5, 4 * n_grp), f32),
            pltpu.VMEM((6, ny5, LANES), f32),
            pltpu.VMEM((2, ny5, LANES), f32),
            pltpu.VMEM((LANES, LANES), f32),
        ]
        + [dma] * 10,
        compiler_params=pltpu.CompilerParams(collective_id=0, has_side_effects=True),
    )(jnp.transpose(residual4, (1, 2, 0)), spacing.reshape(1, LANES))
    correction, coarse = pl.pallas_call(
        hand_over,
        out_shape=(
            jax.ShapeDtypeStruct((4, 4, LANES), f32),
            jax.ShapeDtypeStruct((2, 2, HALF), f32),
        ),
        in_specs=[vmem, vmem],
        out_specs=(anywhere, anywhere),
        scratch_shapes=[dma] * 2,
    )(
        pltpu.with_memory_space_constraint(correction, pltpu.VMEM),
        pltpu.with_memory_space_constraint(coarse, pltpu.VMEM),
    )
    return jnp.transpose(correction, (2, 0, 1)), jnp.transpose(coarse, (2, 0, 1))


def solution(mesh):
    placed = P(None, "grp", "sub")
    return jax.shard_map(
        functools.partial(on_device, mesh.shape["grp"], mesh.shape["sub"]),
        mesh=mesh,
        in_specs=(placed, P()),
        out_specs=(placed, placed),
        check_vma=False,
    )
```

```python
import functools
import math

import jax
import jax.numpy as jnp
from jax import lax
from jax.experimental import pallas as pl
from jax.experimental.pallas import tpu as pltpu
from jax.sharding import PartitionSpec as P

MESH = pl.DeviceIdType.MESH
HIGHEST = lax.Precision.HIGHEST
DAMPING = 0.8
LANES = 128
HALF = 64
REACH = 7


def matmul(left, right):
    return lax.dot_general(
        left, right, (((1,), (0,)), ((), ())), precision=HIGHEST, preferred_element_type=jnp.float32
    )


def iota(shape, axis):
    return lax.broadcasted_iota(jnp.int32, shape, axis).astype(jnp.float32)


def wrapped(value, count):
    return value - count * jnp.floor((value + 0.5) * (1.0 / count))


def cos_turn(step, count):
    step = jnp.minimum(step, count - step)
    flip = step > count / 4
    step = jnp.where(flip, count / 2 - step, step)
    angle = step * (2.0 * math.pi / count)
    sq = angle * angle
    total = jnp.full_like(sq, 1.0 / math.factorial(16))
    for power in range(14, -1, -2):
        sign = 1.0 if power % 4 == 0 else -1.0
        total = total * sq + sign / math.factorial(power)
    return jnp.where(flip, -total, total)


def up_z(field):
    return pltpu.roll(field, LANES - 1, axis=field.ndim - 1)


def down_z(field):
    return pltpu.roll(field, 1, axis=field.ndim - 1)


def operate(rows, south, north, coef):
    height, upper, lower, diagonal = coef
    span = rows.shape[1]
    west = pltpu.roll(rows, 1, axis=1)
    east = pltpu.roll(rows, span - 1, axis=1)
    sides = (west + east) + (south + north)
    return diagonal * rows - height * sides - upper * up_z(rows) - lower * down_z(rows)


def torus(n_sub):
    inner = 8 if n_sub % 8 == 0 else 2
    return n_sub // inner, inner


def ring_hops(step, size):
    return min(step % size, -step % size)


def hops(step, sizes):
    return ring_hops(step[0], sizes[0]) + ring_hops(step[1], sizes[1])


def compose(weights, keep, down, up, step):
    terms = {}
    for offset, weight in weights.items():
        for place, part in (
            (offset, keep * weight),
            (offset - step, down * pltpu.roll(weight, step, axis=1)),
            (offset + step, up * pltpu.roll(weight, LANES - step, axis=1)),
        ):
            terms[place] = terms[place] + part if place in terms else part
    return terms


def owner_places(n_sub):
    outer, inner = torus(n_sub)

    def rank(place):
        step = (place // inner, place % inner)
        return hops(step, (outer, inner)), step[1]

    return sorted(range(n_sub), key=rank)[: n_sub // 2]


def arrived(blocks, semaphore):
    pltpu.make_async_copy(blocks, blocks, semaphore).wait()


def solve_modes(n_grp, n_sub, wave_f, height5, weights_z, still_ref):
    ny5, nx5 = 2 * n_grp, 2 * n_sub
    lane_m = lax.broadcasted_iota(jnp.int32, (ny5, LANES), 1)
    row_m = lax.broadcasted_iota(jnp.int32, (ny5, LANES), 0)
    z5 = lane_m & (HALF - 1)
    z5_8 = z5[0:8]
    face5 = 2.0 / (height5 + up_z(height5))
    upper5 = jnp.where(z5_8 < HALF - 1, face5, 0.0)[0:1]
    lower5 = jnp.where(z5_8 > 0, down_z(face5), 0.0)[0:1]
    height5 = height5[0:1]
    mode = row_m.astype(jnp.float32)
    odd = mode > n_grp
    wave_y = jnp.where(odd, mode - n_grp, mode)
    sin_y = cos_turn(n_grp - wave_y, 2 * ny5)
    wave_x = jnp.where((lane_m >= HALF) & (wave_f == 0.0), 1.0 * n_sub, wave_f)
    sin_x = cos_turn(n_sub - wave_x, 2 * nx5)
    lam = sin_x * sin_x + sin_y * sin_y
    still = (row_m == 0) & (wave_x == 0.0)
    still_ref[...] = jnp.where(still, 1.0, 0.0)
    anchor = jnp.where(still & (z5 == 0), 1.0, 0.0)
    excess = lam * height5 + anchor
    inverse = 1.0 / (excess + upper5 + lower5)
    below = lower5 * inverse
    above = upper5 * inverse
    excess = excess * inverse
    weight = jnp.where(wave_f == 0.0, 1.0 / nx5, 2.0 / nx5)
    terms = {0: inverse}
    for level in range(6):
        step = 1 << level
        below_dn = pltpu.roll(below, step, axis=1)
        above_up = pltpu.roll(above, LANES - step, axis=1)
        excess_dn = pltpu.roll(excess, step, axis=1)
        excess_up = pltpu.roll(excess, LANES - step, axis=1)
        inverse = 1.0 / (excess + below * (below_dn + excess_dn) + above * (above_up + excess_up))
        low, high = below * inverse, above * inverse
        last = weight if level == 5 else 1.0
        keep, down, up = inverse * last, low * last, high * last
        terms = (
            {0: keep, -step: down, step: up} if level == 3 else compose(terms, keep, down, up, step)
        )
        if level % 3 == 2:
            for offset in range(-REACH, REACH + 1):
                weights_z[level // 3, REACH + offset] = terms[offset * (step >> 2)]
        excess = excess * inverse + low * excess_dn + high * excess_up
        below, above = low * below_dn, high * above_up


def transforms(n_grp, forward_ref, backward_ref):
    ny5 = 2 * n_grp
    mode = iota((ny5, LANES), 0)
    odd = mode > n_grp
    wave_y = jnp.where(odd, mode - n_grp, mode)
    shape_f = (ny5, 4 * n_grp)
    mode_f, col_f = iota(shape_f, 0), iota(shape_f, 1)
    chip_f = jnp.floor((col_f + 0.5) * 0.125)
    row_f = wrapped(4.0 * chip_f + (col_f - 8.0 * chip_f) - 1.0, ny5)
    odd_f = mode_f > n_grp
    phase_f = jnp.where(odd_f, mode_f - n_grp, mode_f) * row_f - jnp.where(odd_f, 0.25 * ny5, 0.0)
    forward_ref[...] = cos_turn(wrapped(phase_f, ny5), ny5)
    scale = jnp.where((wave_y == 0.0) | (wave_y == 1.0 * n_grp), 1.0 / ny5, 2.0 / ny5)
    quarter = jnp.where(odd, 0.25 * ny5, 0.0)
    for r in range(6):
        backward_ref[r] = cos_turn(wrapped(wave_y * (r - 1.0) - quarter, ny5), ny5) * scale


def kernel(
    n_grp, n_sub,
    res_hbm, spacing_hbm, cor_ref, coarse_ref,
    res_ref, spacing_ref, pad, table, table8, msg1, recv1, msg2, recv2, msg3, recv3, halo, big, smooth_ref,
    pairs, weights_z, forward_ref, backward_ref, still_ref, spread_ref,
    load1, load2, halo_send, halo_recv, send1, got1, send2, got2, send3, got3,
):
    me_g = lax.axis_index("grp")
    me_s = lax.axis_index("sub")
    ny5, nx5 = 2 * n_grp, 2 * n_sub
    n_z = n_grp // 2
    sizes = torus(n_sub)
    outer, inner = sizes
    me_z, side = me_g // 2, me_g % 2
    owner_g, other_g = 2 * me_z + 1, 2 * me_z

    def moved(step):
        return ((me_s // inner + step[0]) % outer) * inner + (me_s % inner + step[1]) % inner

    places = owner_places(n_sub)
    n_own = len(places)
    own_index = sum(jnp.where(me_s == place, number, 0) for number, place in enumerate(places))
    chosen = sum(jnp.where(me_s == place, 1, 0) for place in places)
    owns = side * chosen == 1

    here = [(a, b) for a in range(outer) for b in range(inner)]
    here.sort(key=lambda step: hops(step, sizes), reverse=True)
    along_z = sorted(range(1, n_z), key=lambda step: ring_hops(step, n_z), reverse=True)
    ring = [(a, b) for a in (0, 1, n_grp - 1) for b in (0, 1, n_sub - 1) if (a, b) != (0, 0)]

    load_res = pltpu.make_async_copy(res_hbm, res_ref, load1)
    load_spacing = pltpu.make_async_copy(spacing_hbm, spacing_ref, load2)
    load_res.start()
    load_spacing.start()
    barrier = pltpu.get_barrier_semaphore()

    def greet(device):
        pl.semaphore_signal(barrier, inc=1, device_id=device, device_id_type=MESH)

    @pl.when(owns)
    def _():
        queue = [(hops(step, sizes), 0, step) for step in here]
        queue += [(hops(step, sizes), 1, step) for step in here if step != (0, 0)]
        queue += [(ring_hops(step, n_z), 2, step) for step in along_z]
        for _, kind, step in sorted(queue, reverse=True):
            if kind == 2:
                greet((2 * ((me_z + step) % n_z) + 1, me_s))
            else:
                greet((owner_g if kind else other_g, moved(step)))

    @pl.when(jnp.logical_not(owns))
    def _():
        for place in places:
            greet((owner_g, place))

    for a, b in ring:
        greet(((me_g + a) % n_grp, (me_s + b) % n_sub))

    shape_t = (n_sub, LANES)
    owner = iota(shape_t, 0)
    second_half = lax.broadcasted_iota(jnp.int32, shape_t, 1) >= HALF
    alone = owner == 0.0
    wave = jnp.where(alone & second_half, 1.0 * n_sub, owner)
    shift = jnp.where(second_half & jnp.logical_not(alone), 0.25 * nx5, 0.0)
    for j in range(4):
        column = wrapped((2 * me_s + (j - 1)).astype(jnp.float32), nx5)
        table[j] = cos_turn(wrapped(wave * column - shift, nx5), nx5)

    load_spacing.wait()
    lane = lax.broadcasted_iota(jnp.int32, (8, LANES), 1)
    height8 = jnp.broadcast_to(spacing_ref[...], (8, LANES))
    face = 2.0 / (height8 + up_z(height8))
    upper8 = jnp.where(lane < LANES - 1, face, 0.0)
    lower8 = jnp.where(lane > 0, down_z(face), 0.0)
    diag8 = 4.0 * height8 + upper8 + lower8
    damp8 = DAMPING / diag8
    coef8 = (height8[None], upper8[None], lower8[None], diag8[None])

    pad[...] = jnp.zeros_like(pad)
    load_res.wait()
    pad[2:6, 2:6, :] = res_ref[...]
    block = pad[...]
    zero_row = jnp.zeros((1, 8, LANES), jnp.float32)

    def operate_zero(rows):
        south = jnp.concatenate([zero_row, rows[:-1]], 0)
        north = jnp.concatenate([rows[1:], zero_row], 0)
        return operate(rows, south, north, coef8)

    first = damp8[None] * block
    second = first + damp8[None] * (block - operate_zero(first))
    leftover = block - operate_zero(second)
    row_pairs = jnp.concatenate([leftover[2 * j] + leftover[2 * j + 1] for j in range(4)], 0)
    z_in = lax.broadcasted_iota(jnp.int32, (LANES, LANES), 0)
    z_out = lax.broadcasted_iota(jnp.int32, (LANES, LANES), 1)
    gather_z = jnp.where((z_in >> 1) == (z_out & (HALF - 1)), 1.0, 0.0)
    pairs[...] = matmul(row_pairs, 0.25 * gather_z)
    parts = [
        pairs[pl.ds(2 * j, 4, stride=8), :] + pairs[pl.ds(2 * j + 1, 4, stride=8), :]
        for j in range(4)
    ]
    for k in range(n_sub):
        total = table[0, k : k + 1, :] * parts[0]
        for j in range(1, 4):
            total = total + table[j, k : k + 1, :] * parts[j]
        msg1[k // 2, 4 * (k % 2) : 4 * (k % 2) + 4, :] = total

    spread_ref[...] = jnp.where((z_out >> 1) == (z_in & (HALF - 1)), 1.0, 0.0)

    pl.semaphore_wait(barrier, 8 + jnp.where(owns, 2 * n_sub - 1 + n_z - 1, n_own))

    def share(number, place):
        pltpu.make_async_remote_copy(
            src_ref=msg1.at[number], dst_ref=recv1.at[side * n_sub + me_s],
            send_sem=send1, recv_sem=got1,
            device_id=(owner_g, place), device_id_type=MESH,
        ).start()

    for number, place in reversed(list(enumerate(places))):
        pl.when(jnp.logical_not(owns) | (me_s != place))(functools.partial(share, number, place))

    for place, (a, b) in enumerate(ring):
        pltpu.make_async_remote_copy(
            src_ref=res_ref, dst_ref=halo.at[place], send_sem=halo_send, recv_sem=halo_recv,
            device_id=((me_g + a) % n_grp, (me_s + b) % n_sub), device_id_type=MESH,
        ).start()

    height5 = matmul(height8, gather_z)

    @pl.when(owns)
    def _():
        recv1[n_sub + me_s] = msg1[own_index]
        transforms(n_grp, forward_ref, backward_ref)
        for pair in range(2):
            wave_f = (2 * own_index + pair).astype(jnp.float32)
            solve_modes(
                n_grp, n_sub, wave_f, height5, weights_z.at[pair], still_ref.at[pair]
            )
        arrived(recv1.at[pl.ds(0, 2 * n_sub - 1)], got1)
        other = jnp.sum(recv1[0:n_sub], axis=0)
        own = jnp.sum(recv1[n_sub : 2 * n_sub], axis=0)
        gap = jnp.zeros((2, LANES), jnp.float32)
        for pair in range(2):
            left, right = other[4 * pair : 4 * pair + 4], own[4 * pair : 4 * pair + 4]
            both = jnp.concatenate([left, gap, gap], 0) + jnp.concatenate([gap, right, gap], 0)
            msg2[pair] = both
            recv2[0, pair] = both
        for step in along_z:
            pltpu.make_async_remote_copy(
                src_ref=msg2, dst_ref=recv2.at[-step % n_z], send_sem=send2, recv_sem=got2,
                device_id=(2 * ((me_z + step) % n_z) + 1, me_s), device_id_type=MESH,
            ).start()
        arrived(recv2.at[pl.ds(1, n_z - 1)], got2)

        fields, means = [], []
        low_half = lax.broadcasted_iota(jnp.int32, (1, LANES), 1) < HALF
        for pair in range(2):
            rows_in = jnp.concatenate([recv2[k, pair] for k in range(n_z)], 0)
            fields.append(matmul(forward_ref[...], rows_in))
            column = jnp.where(low_half, jnp.sum(rows_in, axis=0, keepdims=True), 0.0)
            means.append(jnp.sum(column, axis=1, keepdims=True) * (1.0 / HALF))
        lines = [[], []]
        for pair in range(2):
            field = fields[pair] - still_ref[pair] * means[pair]
            for group in range(2):
                total = weights_z[pair, group, REACH] * field
                for offset in range(1, REACH + 1):
                    step = offset << (3 * group)
                    total = total + (
                        weights_z[pair, group, REACH - offset] * pltpu.roll(field, step, axis=1)
                        + weights_z[pair, group, REACH + offset]
                        * pltpu.roll(field, LANES - step, axis=1)
                    )
                field = total
            for r in range(6):
                line = backward_ref[r, 0:8] * field[0:8]
                for k in range(8, ny5, 8):
                    line = line + backward_ref[r, k : k + 8] * field[k : k + 8]
                lines[pair].append(jnp.sum(line, axis=0, keepdims=True))
        for core, first in ((0, 0), (1, 2)):
            msg3[core] = jnp.concatenate(
                lines[0][first : first + 4] + lines[1][first : first + 4], 0
            )
        recv3[own_index] = msg3[1]

        def give(core, place):
            pltpu.make_async_remote_copy(
                src_ref=msg3.at[core], dst_ref=recv3.at[own_index],
                send_sem=send3, recv_sem=got3,
                device_id=(owner_g if core else other_g, place), device_id_type=MESH,
            ).start()

        in_order = sorted(range(n_sub), key=lambda p: hops((p // inner, p % inner), sizes))
        for place in in_order:
            pl.when(me_s != place)(functools.partial(give, 1, place))
            give(0, place)

    for j in range(4):
        for number in range(n_own):
            table8[j, number] = jnp.concatenate(
                [
                    jnp.broadcast_to(table[j, k : k + 1, :], (4, LANES))
                    for k in (2 * number, 2 * number + 1)
                ],
                0,
            )

    arrived(halo, halo_recv)
    big[:, 12:16, :] = jnp.zeros((12, 4, LANES), jnp.float32)
    big[4:8, 4:8, :] = res_ref[...]
    for place, (a, b) in enumerate(ring):
        at_y = {0: 4, 1: 0, n_grp - 1: 8}[a]
        at_x = {0: 4, 1: 0, n_sub - 1: 8}[b]
        big[at_y : at_y + 4, at_x : at_x + 4, :] = halo[place]
    wide = big[...]
    coef1 = tuple(value[:, 0:1] for value in coef8)
    damp1 = damp8[None, 0:1]
    first_w = damp1 * wide
    inner_w = first_w[1:-1] + damp1 * (
        wide[1:-1] - operate(first_w[1:-1], first_w[:-2], first_w[2:], coef1)
    )
    smooth_ref[...] = inner_w[1:-1]
    smooth = smooth_ref[:, 2:10, :]
    near = big[2:10, 2:10, :]

    @pl.when(owns)
    def _():
        arrived(recv3.at[pl.ds(0, n_own - 1)], got3)

    @pl.when(jnp.logical_not(owns))
    def _():
        arrived(recv3, got3)

    for j in range(4):
        total = table8[j, 0] * recv3[0]
        for k in range(1, n_own):
            total = total + table8[j, k] * recv3[k]
        total = total[0:4] + total[4:8]
        pairs[pl.ds(2 * j, 4, stride=8), :] = total
        pairs[pl.ds(2 * j + 1, 4, stride=8), :] = total
    for j in (1, 2):
        both = pairs[pl.ds(8 * j + 2, 2, stride=2), :]
        coarse_ref[j - 1] = (both + pltpu.roll(both, HALF, axis=1))[:, 0:HALF]
    coarse = matmul(pairs[...], spread_ref[...])
    lifted = smooth + jnp.concatenate(
        [coarse[8 * (j // 2) : 8 * (j // 2) + 8][None] for j in range(8)], 0
    )
    lifted = lifted[1:-1] + damp8[None] * (
        near[1:-1] - operate(lifted[1:-1], lifted[:-2], lifted[2:], coef8)
    )
    lifted = lifted[1:-1] + damp8[None] * (
        near[2:-2] - operate(lifted[1:-1], lifted[:-2], lifted[2:], coef8)
    )
    cor_ref[...] = lifted[:, 2:6, :]

    arrived(halo, halo_send)

    @pl.when(owns)
    def _():
        arrived(recv1.at[pl.ds(0, n_own - 1)], send1)
        arrived(recv2.at[pl.ds(1, n_z - 1)], send2)
        arrived(recv1.at[pl.ds(0, 2 * n_sub - 1)], send3)

    @pl.when(jnp.logical_not(owns))
    def _():
        arrived(recv1.at[pl.ds(0, n_own)], send1)


def hand_over(cor_in, coarse_in, cor_out, coarse_out, sem1, sem2):
    first = pltpu.make_async_copy(cor_in, cor_out, sem1)
    second = pltpu.make_async_copy(coarse_in, coarse_out, sem2)
    first.start()
    second.start()
    first.wait()
    second.wait()


def on_device(n_grp, n_sub, residual4, spacing):
    f32 = jnp.float32
    ny5 = 2 * n_grp
    dma = pltpu.SemaphoreType.DMA
    vmem = pl.BlockSpec(memory_space=pltpu.VMEM)
    anywhere = pl.BlockSpec(memory_space=pl.ANY)
    correction, coarse = pl.pallas_call(
        functools.partial(kernel, n_grp, n_sub),
        out_shape=(
            pltpu.VMEM((4, 4, LANES), f32),
            pltpu.VMEM((2, 2, HALF), f32),
        ),
        in_specs=[anywhere, anywhere],
        out_specs=(vmem, vmem),
        scratch_shapes=[
            pltpu.VMEM((4, 4, LANES), f32),
            pltpu.VMEM((1, LANES), f32),
            pltpu.VMEM((8, 8, LANES), f32),
            pltpu.VMEM((4, n_sub, LANES), f32),
            pltpu.VMEM((4, n_sub // 2, 8, LANES), f32),
            pltpu.VMEM((n_sub // 2, 8, LANES), f32),
            pltpu.VMEM((2 * n_sub, 8, LANES), f32),
            pltpu.VMEM((2, 8, LANES), f32),
            pltpu.VMEM((n_grp // 2, 2, 8, LANES), f32),
            pltpu.VMEM((2, 8, LANES), f32),
            pltpu.VMEM((n_sub // 2, 8, LANES), f32),
            pltpu.VMEM((8, 4, 4, LANES), f32),
            pltpu.VMEM((12, 16, LANES), f32),
            pltpu.VMEM((8, 16, LANES), f32),
            pltpu.VMEM((32, LANES), f32),
            pltpu.VMEM((2, 2, 2 * REACH + 1, ny5, LANES), f32),
            pltpu.VMEM((ny5, 4 * n_grp), f32),
            pltpu.VMEM((6, ny5, LANES), f32),
            pltpu.VMEM((2, ny5, LANES), f32),
            pltpu.VMEM((LANES, LANES), f32),
        ]
        + [dma] * 10,
        compiler_params=pltpu.CompilerParams(collective_id=0, has_side_effects=True),
    )(jnp.transpose(residual4, (1, 2, 0)), spacing.reshape(1, LANES))
    correction, coarse = pl.pallas_call(
        hand_over,
        out_shape=(
            jax.ShapeDtypeStruct((4, 4, LANES), f32),
            jax.ShapeDtypeStruct((2, 2, HALF), f32),
        ),
        in_specs=[vmem, vmem],
        out_specs=(anywhere, anywhere),
        scratch_shapes=[dma] * 2,
    )(
        pltpu.with_memory_space_constraint(correction, pltpu.VMEM),
        pltpu.with_memory_space_constraint(coarse, pltpu.VMEM),
    )
    return jnp.transpose(correction, (2, 0, 1)), jnp.transpose(coarse, (2, 0, 1))


def solution(mesh):
    placed = P(None, "grp", "sub")
    return jax.shard_map(
        functools.partial(on_device, mesh.shape["grp"], mesh.shape["sub"]),
        mesh=mesh,
        in_specs=(placed, P()),
        out_specs=(placed, placed),
        check_vma=False,
    )
```

```python
import functools
import math

import jax
import jax.numpy as jnp
from jax import lax
from jax.experimental import pallas as pl
from jax.experimental.pallas import tpu as pltpu
from jax.sharding import PartitionSpec as P

MESH = pl.DeviceIdType.MESH
HIGHEST = lax.Precision.HIGHEST
DAMPING = 0.8
LANES = 128
HALF = 64
REACH = 7


def matmul(left, right):
    return lax.dot_general(
        left, right, (((1,), (0,)), ((), ())), precision=HIGHEST, preferred_element_type=jnp.float32
    )


def iota(shape, axis):
    return lax.broadcasted_iota(jnp.int32, shape, axis).astype(jnp.float32)


def wrapped(value, count):
    return value - count * jnp.floor((value + 0.5) * (1.0 / count))


def cos_turn(step, count):
    step = jnp.minimum(step, count - step)
    flip = step > count / 4
    step = jnp.where(flip, count / 2 - step, step)
    angle = step * (2.0 * math.pi / count)
    sq = angle * angle
    total = jnp.full_like(sq, 1.0 / math.factorial(16))
    for power in range(14, -1, -2):
        sign = 1.0 if power % 4 == 0 else -1.0
        total = total * sq + sign / math.factorial(power)
    return jnp.where(flip, -total, total)


def up_z(field):
    return pltpu.roll(field, LANES - 1, axis=field.ndim - 1)


def down_z(field):
    return pltpu.roll(field, 1, axis=field.ndim - 1)


def operate(rows, south, north, coef):
    height, upper, lower, diagonal = coef
    span = rows.shape[1]
    west = pltpu.roll(rows, 1, axis=1)
    east = pltpu.roll(rows, span - 1, axis=1)
    sides = (west + east) + (south + north)
    return diagonal * rows - height * sides - upper * up_z(rows) - lower * down_z(rows)


def torus(n_sub):
    inner = 8 if n_sub % 8 == 0 else 2
    return n_sub // inner, inner


def ring_hops(step, size):
    return min(step % size, -step % size)


def hops(step, sizes):
    return ring_hops(step[0], sizes[0]) + ring_hops(step[1], sizes[1])


def compose(weights, keep, down, up, step):
    terms = {}
    for offset, weight in weights.items():
        for place, part in (
            (offset, keep * weight),
            (offset - step, down * pltpu.roll(weight, step, axis=1)),
            (offset + step, up * pltpu.roll(weight, LANES - step, axis=1)),
        ):
            terms[place] = terms[place] + part if place in terms else part
    return terms


def owner_places(n_sub):
    outer, inner = torus(n_sub)

    def rank(place):
        step = (place // inner, place % inner)
        return hops(step, (outer, inner)), step[1]

    return sorted(range(n_sub), key=rank)[: n_sub // 2]


def arrived(blocks, semaphore):
    pltpu.make_async_copy(blocks, blocks, semaphore).wait()


def solve_modes(n_grp, n_sub, wave_f, height5, weights_z, still_ref):
    ny5, nx5 = 2 * n_grp, 2 * n_sub
    lane_m = lax.broadcasted_iota(jnp.int32, (ny5, LANES), 1)
    row_m = lax.broadcasted_iota(jnp.int32, (ny5, LANES), 0)
    z5 = lane_m & (HALF - 1)
    z5_8 = z5[0:8]
    face5 = 2.0 / (height5 + up_z(height5))
    upper5 = jnp.where(z5_8 < HALF - 1, face5, 0.0)[0:1]
    lower5 = jnp.where(z5_8 > 0, down_z(face5), 0.0)[0:1]
    height5 = height5[0:1]
    mode = row_m.astype(jnp.float32)
    odd = mode > n_grp
    wave_y = jnp.where(odd, mode - n_grp, mode)
    sin_y = cos_turn(n_grp - wave_y, 2 * ny5)
    wave_x = jnp.where((lane_m >= HALF) & (wave_f == 0.0), 1.0 * n_sub, wave_f)
    sin_x = cos_turn(n_sub - wave_x, 2 * nx5)
    lam = sin_x * sin_x + sin_y * sin_y
    still = (row_m == 0) & (wave_x == 0.0)
    still_ref[...] = jnp.where(still, 1.0, 0.0)
    anchor = jnp.where(still & (z5 == 0), 1.0, 0.0)
    excess = lam * height5 + anchor
    inverse = 1.0 / (excess + upper5 + lower5)
    below = lower5 * inverse
    above = upper5 * inverse
    excess = excess * inverse
    weight = jnp.where(wave_f == 0.0, 1.0 / nx5, 2.0 / nx5)
    terms = {0: inverse}
    for level in range(6):
        step = 1 << level
        below_dn = pltpu.roll(below, step, axis=1)
        above_up = pltpu.roll(above, LANES - step, axis=1)
        excess_dn = pltpu.roll(excess, step, axis=1)
        excess_up = pltpu.roll(excess, LANES - step, axis=1)
        inverse = 1.0 / (excess + below * (below_dn + excess_dn) + above * (above_up + excess_up))
        low, high = below * inverse, above * inverse
        last = weight if level == 5 else 1.0
        keep, down, up = inverse * last, low * last, high * last
        terms = (
            {0: keep, -step: down, step: up} if level == 3 else compose(terms, keep, down, up, step)
        )
        if level % 3 == 2:
            for offset in range(-REACH, REACH + 1):
                weights_z[level // 3, REACH + offset] = terms[offset * (step >> 2)]
        excess = excess * inverse + low * excess_dn + high * excess_up
        below, above = low * below_dn, high * above_up


def transforms(n_grp, forward_ref, backward_ref):
    ny5 = 2 * n_grp
    mode = iota((ny5, LANES), 0)
    odd = mode > n_grp
    wave_y = jnp.where(odd, mode - n_grp, mode)
    shape_f = (ny5, 4 * n_grp)
    mode_f, col_f = iota(shape_f, 0), iota(shape_f, 1)
    chip_f = jnp.floor((col_f + 0.5) * 0.125)
    row_f = wrapped(4.0 * chip_f + (col_f - 8.0 * chip_f) - 1.0, ny5)
    odd_f = mode_f > n_grp
    phase_f = jnp.where(odd_f, mode_f - n_grp, mode_f) * row_f - jnp.where(odd_f, 0.25 * ny5, 0.0)
    forward_ref[...] = cos_turn(wrapped(phase_f, ny5), ny5)
    scale = jnp.where((wave_y == 0.0) | (wave_y == 1.0 * n_grp), 1.0 / ny5, 2.0 / ny5)
    quarter = jnp.where(odd, 0.25 * ny5, 0.0)
    for r in range(6):
        backward_ref[r] = cos_turn(wrapped(wave_y * (r - 1.0) - quarter, ny5), ny5) * scale


def kernel(
    n_grp, n_sub,
    res_hbm, spacing_hbm, cor_ref, coarse_ref,
    res_ref, spacing_ref, pad, table, table8, msg1, recv1, msg2, recv2, msg3, recv3, halo, big, smooth_ref,
    pairs, weights_z, forward_ref, backward_ref, still_ref, spread_ref,
    load1, load2, halo_send, halo_recv, send1, got1, send2, got2, send3, got3,
):
    me_g = lax.axis_index("grp")
    me_s = lax.axis_index("sub")
    ny5, nx5 = 2 * n_grp, 2 * n_sub
    n_z = n_grp // 2
    sizes = torus(n_sub)
    outer, inner = sizes
    me_z, side = me_g // 2, me_g % 2
    owner_g, other_g = 2 * me_z + 1, 2 * me_z

    def moved(step):
        return ((me_s // inner + step[0]) % outer) * inner + (me_s % inner + step[1]) % inner

    places = owner_places(n_sub)
    n_own = len(places)
    own_index = sum(jnp.where(me_s == place, number, 0) for number, place in enumerate(places))
    chosen = sum(jnp.where(me_s == place, 1, 0) for place in places)
    owns = side * chosen == 1

    here = [(a, b) for a in range(outer) for b in range(inner)]
    here.sort(key=lambda step: hops(step, sizes), reverse=True)
    along_z = sorted(range(1, n_z), key=lambda step: ring_hops(step, n_z), reverse=True)
    ring = [(a, b) for a in (0, 1, n_grp - 1) for b in (0, 1, n_sub - 1) if (a, b) != (0, 0)]

    load_res = pltpu.make_async_copy(res_hbm, res_ref, load1)
    load_spacing = pltpu.make_async_copy(spacing_hbm, spacing_ref, load2)
    load_res.start()
    load_spacing.start()
    barrier = pltpu.get_barrier_semaphore()

    def greet(device):
        pl.semaphore_signal(barrier, inc=1, device_id=device, device_id_type=MESH)

    @pl.when(owns)
    def _():
        queue = [(hops(step, sizes), 0, step) for step in here]
        queue += [(hops(step, sizes), 1, step) for step in here if step != (0, 0)]
        queue += [(ring_hops(step, n_z), 2, step) for step in along_z]
        for _, kind, step in sorted(queue, reverse=True):
            if kind == 2:
                greet((2 * ((me_z + step) % n_z) + 1, me_s))
            else:
                greet((owner_g if kind else other_g, moved(step)))

    @pl.when(jnp.logical_not(owns))
    def _():
        for place in places:
            greet((owner_g, place))

    for a, b in ring:
        greet(((me_g + a) % n_grp, (me_s + b) % n_sub))

    shape_t = (n_sub, LANES)
    owner = iota(shape_t, 0)
    second_half = lax.broadcasted_iota(jnp.int32, shape_t, 1) >= HALF
    alone = owner == 0.0
    wave = jnp.where(alone & second_half, 1.0 * n_sub, owner)
    shift = jnp.where(second_half & jnp.logical_not(alone), 0.25 * nx5, 0.0)
    for j in range(4):
        column = wrapped((2 * me_s + (j - 1)).astype(jnp.float32), nx5)
        table[j] = cos_turn(wrapped(wave * column - shift, nx5), nx5)

    load_spacing.wait()
    lane = lax.broadcasted_iota(jnp.int32, (8, LANES), 1)
    height8 = jnp.broadcast_to(spacing_ref[...], (8, LANES))
    face = 2.0 / (height8 + up_z(height8))
    upper8 = jnp.where(lane < LANES - 1, face, 0.0)
    lower8 = jnp.where(lane > 0, down_z(face), 0.0)
    diag8 = 4.0 * height8 + upper8 + lower8
    damp8 = DAMPING / diag8
    coef8 = (height8[None], upper8[None], lower8[None], diag8[None])

    pad[...] = jnp.zeros_like(pad)
    load_res.wait()
    pad[2:6, 2:6, :] = res_ref[...]
    block = pad[...]
    zero_row = jnp.zeros((1, 8, LANES), jnp.float32)

    def operate_zero(rows):
        south = jnp.concatenate([zero_row, rows[:-1]], 0)
        north = jnp.concatenate([rows[1:], zero_row], 0)
        return operate(rows, south, north, coef8)

    first = damp8[None] * block
    second = first + damp8[None] * (block - operate_zero(first))
    leftover = block - operate_zero(second)
    row_pairs = jnp.concatenate([leftover[2 * j] + leftover[2 * j + 1] for j in range(4)], 0)
    z_in = lax.broadcasted_iota(jnp.int32, (LANES, LANES), 0)
    z_out = lax.broadcasted_iota(jnp.int32, (LANES, LANES), 1)
    gather_z = jnp.where((z_in >> 1) == (z_out & (HALF - 1)), 1.0, 0.0)
    pairs[...] = matmul(row_pairs, 0.25 * gather_z)
    parts = [
        pairs[pl.ds(2 * j, 4, stride=8), :] + pairs[pl.ds(2 * j + 1, 4, stride=8), :]
        for j in range(4)
    ]
    for k in range(n_sub):
        total = table[0, k : k + 1, :] * parts[0]
        for j in range(1, 4):
            total = total + table[j, k : k + 1, :] * parts[j]
        msg1[k // 2, 4 * (k % 2) : 4 * (k % 2) + 4, :] = total

    spread_ref[...] = jnp.where((z_out >> 1) == (z_in & (HALF - 1)), 1.0, 0.0)

    pl.semaphore_wait(barrier, 8 + jnp.where(owns, 2 * n_sub - 1 + n_z - 1, n_own))

    def share(number, place):
        pltpu.make_async_remote_copy(
            src_ref=msg1.at[number], dst_ref=recv1.at[side * n_sub + me_s],
            send_sem=send1, recv_sem=got1,
            device_id=(owner_g, place), device_id_type=MESH,
        ).start()

    behind = (0.0, 0.4, 0.8, 1.2, 1.8, 1.7, 1.3, 1.1)

    def start_of(item):
        return 0.6 * ring_hops(item[1] // inner, outer) + behind[item[1] % 8]

    for number, place in sorted(enumerate(places), key=start_of, reverse=True):
        pl.when(jnp.logical_not(owns) | (me_s != place))(functools.partial(share, number, place))

    for place, (a, b) in enumerate(ring):
        pltpu.make_async_remote_copy(
            src_ref=res_ref, dst_ref=halo.at[place], send_sem=halo_send, recv_sem=halo_recv,
            device_id=((me_g + a) % n_grp, (me_s + b) % n_sub), device_id_type=MESH,
        ).start()

    height5 = matmul(height8, gather_z)

    @pl.when(owns)
    def _():
        recv1[n_sub + me_s] = msg1[own_index]
        transforms(n_grp, forward_ref, backward_ref)
        for pair in range(2):
            wave_f = (2 * own_index + pair).astype(jnp.float32)
            solve_modes(
                n_grp, n_sub, wave_f, height5, weights_z.at[pair], still_ref.at[pair]
            )
        arrived(recv1.at[pl.ds(0, 2 * n_sub - 1)], got1)
        other = jnp.sum(recv1[0:n_sub], axis=0)
        own = jnp.sum(recv1[n_sub : 2 * n_sub], axis=0)
        gap = jnp.zeros((2, LANES), jnp.float32)
        for pair in range(2):
            left, right = other[4 * pair : 4 * pair + 4], own[4 * pair : 4 * pair + 4]
            both = jnp.concatenate([left, gap, gap], 0) + jnp.concatenate([gap, right, gap], 0)
            msg2[pair] = both
            recv2[0, pair] = both
        for step in along_z:
            pltpu.make_async_remote_copy(
                src_ref=msg2, dst_ref=recv2.at[-step % n_z], send_sem=send2, recv_sem=got2,
                device_id=(2 * ((me_z + step) % n_z) + 1, me_s), device_id_type=MESH,
            ).start()
        arrived(recv2.at[pl.ds(1, n_z - 1)], got2)

        fields, means = [], []
        low_half = lax.broadcasted_iota(jnp.int32, (1, LANES), 1) < HALF
        rows_in = jnp.concatenate(
            [
                jnp.concatenate([recv2[k, pair] for k in range(n_z)], 0)
                for pair in range(2)
            ],
            1,
        )
        spectrum = matmul(forward_ref[...], rows_in)
        for pair in range(2):
            half = slice(LANES * pair, LANES * (pair + 1))
            fields.append(spectrum[:, half])
            column = jnp.where(low_half, jnp.sum(rows_in[:, half], axis=0, keepdims=True), 0.0)
            means.append(jnp.sum(column, axis=1, keepdims=True) * (1.0 / HALF))
        lines = [[], []]
        for pair in range(2):
            field = fields[pair] - still_ref[pair] * means[pair]
            for group in range(2):
                total = weights_z[pair, group, REACH] * field
                for offset in range(1, REACH + 1):
                    step = offset << (3 * group)
                    total = total + (
                        weights_z[pair, group, REACH - offset] * pltpu.roll(field, step, axis=1)
                        + weights_z[pair, group, REACH + offset]
                        * pltpu.roll(field, LANES - step, axis=1)
                    )
                field = total
            for r in range(6):
                line = backward_ref[r, 0:8] * field[0:8]
                for k in range(8, ny5, 8):
                    line = line + backward_ref[r, k : k + 8] * field[k : k + 8]
                lines[pair].append(jnp.sum(line, axis=0, keepdims=True))
        for core, first in ((0, 0), (1, 2)):
            msg3[core] = jnp.concatenate(
                lines[0][first : first + 4] + lines[1][first : first + 4], 0
            )
        recv3[own_index] = msg3[1]

        def give(core, place):
            pltpu.make_async_remote_copy(
                src_ref=msg3.at[core], dst_ref=recv3.at[own_index],
                send_sem=send3, recv_sem=got3,
                device_id=(owner_g if core else other_g, place), device_id_type=MESH,
            ).start()

        in_order = sorted(range(n_sub), key=lambda p: hops((p // inner, p % inner), sizes))
        for place in in_order:
            pl.when(me_s != place)(functools.partial(give, 1, place))
            give(0, place)

    for j in range(4):
        for number in range(n_own):
            table8[j, number] = jnp.concatenate(
                [
                    jnp.broadcast_to(table[j, k : k + 1, :], (4, LANES))
                    for k in (2 * number, 2 * number + 1)
                ],
                0,
            )

    arrived(halo, halo_recv)
    big[:, 12:16, :] = jnp.zeros((12, 4, LANES), jnp.float32)
    big[4:8, 4:8, :] = res_ref[...]
    for place, (a, b) in enumerate(ring):
        at_y = {0: 4, 1: 0, n_grp - 1: 8}[a]
        at_x = {0: 4, 1: 0, n_sub - 1: 8}[b]
        big[at_y : at_y + 4, at_x : at_x + 4, :] = halo[place]
    wide = big[...]
    coef1 = tuple(value[:, 0:1] for value in coef8)
    damp1 = damp8[None, 0:1]
    first_w = damp1 * wide
    inner_w = first_w[1:-1] + damp1 * (
        wide[1:-1] - operate(first_w[1:-1], first_w[:-2], first_w[2:], coef1)
    )
    smooth_ref[...] = inner_w[1:-1]
    smooth = smooth_ref[:, 2:10, :]
    near = big[2:10, 2:10, :]

    @pl.when(owns)
    def _():
        arrived(recv3.at[pl.ds(0, n_own - 1)], got3)

    @pl.when(jnp.logical_not(owns))
    def _():
        arrived(recv3, got3)

    for j in range(4):
        total = table8[j, 0] * recv3[0]
        for k in range(1, n_own):
            total = total + table8[j, k] * recv3[k]
        total = total[0:4] + total[4:8]
        pairs[pl.ds(2 * j, 4, stride=8), :] = total
        pairs[pl.ds(2 * j + 1, 4, stride=8), :] = total
    for j in (1, 2):
        both = pairs[pl.ds(8 * j + 2, 2, stride=2), :]
        coarse_ref[j - 1] = (both + pltpu.roll(both, HALF, axis=1))[:, 0:HALF]
    coarse = matmul(pairs[...], spread_ref[...])
    lifted = smooth + jnp.concatenate(
        [coarse[8 * (j // 2) : 8 * (j // 2) + 8][None] for j in range(8)], 0
    )
    lifted = lifted[1:-1] + damp8[None] * (
        near[1:-1] - operate(lifted[1:-1], lifted[:-2], lifted[2:], coef8)
    )
    lifted = lifted[1:-1] + damp8[None] * (
        near[2:-2] - operate(lifted[1:-1], lifted[:-2], lifted[2:], coef8)
    )
    cor_ref[...] = lifted[:, 2:6, :]

    arrived(halo, halo_send)

    @pl.when(owns)
    def _():
        arrived(recv1.at[pl.ds(0, n_own - 1)], send1)
        arrived(recv2.at[pl.ds(1, n_z - 1)], send2)
        arrived(recv1.at[pl.ds(0, 2 * n_sub - 1)], send3)

    @pl.when(jnp.logical_not(owns))
    def _():
        arrived(recv1.at[pl.ds(0, n_own)], send1)


def hand_over(cor_in, coarse_in, cor_out, coarse_out, sem1, sem2):
    first = pltpu.make_async_copy(cor_in, cor_out, sem1)
    second = pltpu.make_async_copy(coarse_in, coarse_out, sem2)
    first.start()
    second.start()
    first.wait()
    second.wait()


def on_device(n_grp, n_sub, residual4, spacing):
    f32 = jnp.float32
    ny5 = 2 * n_grp
    dma = pltpu.SemaphoreType.DMA
    vmem = pl.BlockSpec(memory_space=pltpu.VMEM)
    anywhere = pl.BlockSpec(memory_space=pl.ANY)
    correction, coarse = pl.pallas_call(
        functools.partial(kernel, n_grp, n_sub),
        out_shape=(
            pltpu.VMEM((4, 4, LANES), f32),
            pltpu.VMEM((2, 2, HALF), f32),
        ),
        in_specs=[anywhere, anywhere],
        out_specs=(vmem, vmem),
        scratch_shapes=[
            pltpu.VMEM((4, 4, LANES), f32),
            pltpu.VMEM((1, LANES), f32),
            pltpu.VMEM((8, 8, LANES), f32),
            pltpu.VMEM((4, n_sub, LANES), f32),
            pltpu.VMEM((4, n_sub // 2, 8, LANES), f32),
            pltpu.VMEM((n_sub // 2, 8, LANES), f32),
            pltpu.VMEM((2 * n_sub, 8, LANES), f32),
            pltpu.VMEM((2, 8, LANES), f32),
            pltpu.VMEM((n_grp // 2, 2, 8, LANES), f32),
            pltpu.VMEM((2, 8, LANES), f32),
            pltpu.VMEM((n_sub // 2, 8, LANES), f32),
            pltpu.VMEM((8, 4, 4, LANES), f32),
            pltpu.VMEM((12, 16, LANES), f32),
            pltpu.VMEM((8, 16, LANES), f32),
            pltpu.VMEM((32, LANES), f32),
            pltpu.VMEM((2, 2, 2 * REACH + 1, ny5, LANES), f32),
            pltpu.VMEM((ny5, 4 * n_grp), f32),
            pltpu.VMEM((6, ny5, LANES), f32),
            pltpu.VMEM((2, ny5, LANES), f32),
            pltpu.VMEM((LANES, LANES), f32),
        ]
        + [dma] * 10,
        compiler_params=pltpu.CompilerParams(collective_id=0, has_side_effects=True),
    )(jnp.transpose(residual4, (1, 2, 0)), spacing.reshape(1, LANES))
    correction, coarse = pl.pallas_call(
        hand_over,
        out_shape=(
            jax.ShapeDtypeStruct((4, 4, LANES), f32),
            jax.ShapeDtypeStruct((2, 2, HALF), f32),
        ),
        in_specs=[vmem, vmem],
        out_specs=(anywhere, anywhere),
        scratch_shapes=[dma] * 2,
    )(
        pltpu.with_memory_space_constraint(correction, pltpu.VMEM),
        pltpu.with_memory_space_constraint(coarse, pltpu.VMEM),
    )
    return jnp.transpose(correction, (2, 0, 1)), jnp.transpose(coarse, (2, 0, 1))


def solution(mesh):
    placed = P(None, "grp", "sub")
    return jax.shard_map(
        functools.partial(on_device, mesh.shape["grp"], mesh.shape["sub"]),
        mesh=mesh,
        in_specs=(placed, P()),
        out_specs=(placed, placed),
        check_vma=False,
    )
```

```python
import functools
import math

import jax
import jax.numpy as jnp
from jax import lax
from jax.experimental import pallas as pl
from jax.experimental.pallas import tpu as pltpu
from jax.sharding import PartitionSpec as P

MESH = pl.DeviceIdType.MESH
HIGHEST = lax.Precision.HIGHEST
DAMPING = 0.8
LANES = 128
HALF = 64
REACH = 7


def matmul(left, right):
    return lax.dot_general(
        left, right, (((1,), (0,)), ((), ())), precision=HIGHEST, preferred_element_type=jnp.float32
    )


def iota(shape, axis):
    return lax.broadcasted_iota(jnp.int32, shape, axis).astype(jnp.float32)


def wrapped(value, count):
    return value - count * jnp.floor((value + 0.5) * (1.0 / count))


def cos_turn(step, count):
    step = jnp.minimum(step, count - step)
    flip = step > count / 4
    step = jnp.where(flip, count / 2 - step, step)
    angle = step * (2.0 * math.pi / count)
    sq = angle * angle
    total = jnp.full_like(sq, 1.0 / math.factorial(16))
    for power in range(14, -1, -2):
        sign = 1.0 if power % 4 == 0 else -1.0
        total = total * sq + sign / math.factorial(power)
    return jnp.where(flip, -total, total)


def up_z(field):
    return pltpu.roll(field, LANES - 1, axis=field.ndim - 1)


def down_z(field):
    return pltpu.roll(field, 1, axis=field.ndim - 1)


def operate(rows, south, north, coef):
    height, upper, lower, diagonal = coef
    span = rows.shape[1]
    west = pltpu.roll(rows, 1, axis=1)
    east = pltpu.roll(rows, span - 1, axis=1)
    sides = (west + east) + (south + north)
    return diagonal * rows - height * sides - upper * up_z(rows) - lower * down_z(rows)


def torus(n_sub):
    inner = 8 if n_sub % 8 == 0 else 2
    return n_sub // inner, inner


def ring_hops(step, size):
    return min(step % size, -step % size)


def hops(step, sizes):
    return ring_hops(step[0], sizes[0]) + ring_hops(step[1], sizes[1])


def compose(weights, keep, down, up, step):
    terms = {}
    for offset, weight in weights.items():
        for place, part in (
            (offset, keep * weight),
            (offset - step, down * pltpu.roll(weight, step, axis=1)),
            (offset + step, up * pltpu.roll(weight, LANES - step, axis=1)),
        ):
            terms[place] = terms[place] + part if place in terms else part
    return terms


def owner_places(n_sub):
    outer, inner = torus(n_sub)

    def rank(place):
        step = (place // inner, place % inner)
        return hops(step, (outer, inner)), step[1]

    return sorted(range(n_sub), key=rank)[: n_sub // 2]


def arrived(blocks, semaphore):
    pltpu.make_async_copy(blocks, blocks, semaphore).wait()


def solve_modes(n_grp, n_sub, wave_f, height5, weights_z, still_ref):
    ny5, nx5 = 2 * n_grp, 2 * n_sub
    lane_m = lax.broadcasted_iota(jnp.int32, (ny5, LANES), 1)
    row_m = lax.broadcasted_iota(jnp.int32, (ny5, LANES), 0)
    z5 = lane_m & (HALF - 1)
    z5_8 = z5[0:8]
    face5 = 2.0 / (height5 + up_z(height5))
    upper5 = jnp.where(z5_8 < HALF - 1, face5, 0.0)[0:1]
    lower5 = jnp.where(z5_8 > 0, down_z(face5), 0.0)[0:1]
    height5 = height5[0:1]
    mode = row_m.astype(jnp.float32)
    odd = mode > n_grp
    wave_y = jnp.where(odd, mode - n_grp, mode)
    sin_y = cos_turn(n_grp - wave_y, 2 * ny5)
    wave_x = jnp.where((lane_m >= HALF) & (wave_f == 0.0), 1.0 * n_sub, wave_f)
    sin_x = cos_turn(n_sub - wave_x, 2 * nx5)
    lam = sin_x * sin_x + sin_y * sin_y
    still = (row_m == 0) & (wave_x == 0.0)
    still_ref[...] = jnp.where(still, 1.0, 0.0)
    anchor = jnp.where(still & (z5 == 0), 1.0, 0.0)
    excess = lam * height5 + anchor
    inverse = 1.0 / (excess + upper5 + lower5)
    below = lower5 * inverse
    above = upper5 * inverse
    excess = excess * inverse
    weight = jnp.where(wave_f == 0.0, 1.0 / nx5, 2.0 / nx5)
    terms = {0: inverse}
    for level in range(6):
        step = 1 << level
        below_dn = pltpu.roll(below, step, axis=1)
        above_up = pltpu.roll(above, LANES - step, axis=1)
        excess_dn = pltpu.roll(excess, step, axis=1)
        excess_up = pltpu.roll(excess, LANES - step, axis=1)
        inverse = 1.0 / (excess + below * (below_dn + excess_dn) + above * (above_up + excess_up))
        low, high = below * inverse, above * inverse
        last = weight if level == 5 else 1.0
        keep, down, up = inverse * last, low * last, high * last
        terms = (
            {0: keep, -step: down, step: up} if level == 3 else compose(terms, keep, down, up, step)
        )
        if level % 3 == 2:
            for offset in range(-REACH, REACH + 1):
                weights_z[level // 3, REACH + offset] = terms[offset * (step >> 2)]
        excess = excess * inverse + low * excess_dn + high * excess_up
        below, above = low * below_dn, high * above_up


def transforms(n_grp, forward_ref, backward_ref):
    ny5 = 2 * n_grp
    mode = iota((ny5, LANES), 0)
    odd = mode > n_grp
    wave_y = jnp.where(odd, mode - n_grp, mode)
    shape_f = (ny5, 4 * n_grp)
    mode_f, col_f = iota(shape_f, 0), iota(shape_f, 1)
    chip_f = jnp.floor((col_f + 0.5) * 0.125)
    row_f = wrapped(4.0 * chip_f + (col_f - 8.0 * chip_f) - 1.0, ny5)
    odd_f = mode_f > n_grp
    phase_f = jnp.where(odd_f, mode_f - n_grp, mode_f) * row_f - jnp.where(odd_f, 0.25 * ny5, 0.0)
    forward_ref[...] = cos_turn(wrapped(phase_f, ny5), ny5)
    scale = jnp.where((wave_y == 0.0) | (wave_y == 1.0 * n_grp), 1.0 / ny5, 2.0 / ny5)
    quarter = jnp.where(odd, 0.25 * ny5, 0.0)
    for r in range(6):
        backward_ref[r] = cos_turn(wrapped(wave_y * (r - 1.0) - quarter, ny5), ny5) * scale


def kernel(
    n_grp, n_sub,
    res_hbm, spacing_hbm, cor_ref, coarse_ref,
    res_ref, spacing_ref, pad, table, table8, msg1, recv1, msg2, recv2, msg3, recv3, halo, big, smooth_ref,
    pairs, weights_z, forward_ref, backward_ref, still_ref, spread_ref,
    load1, load2, halo_send, halo_recv, send1, got1, send2, got2, send3, got3,
):
    me_g = lax.axis_index("grp")
    me_s = lax.axis_index("sub")
    ny5, nx5 = 2 * n_grp, 2 * n_sub
    n_z = n_grp // 2
    sizes = torus(n_sub)
    outer, inner = sizes
    me_z, side = me_g // 2, me_g % 2
    owner_g, other_g = 2 * me_z + 1, 2 * me_z

    def moved(step):
        return ((me_s // inner + step[0]) % outer) * inner + (me_s % inner + step[1]) % inner

    places = owner_places(n_sub)
    n_own = len(places)
    own_index = sum(jnp.where(me_s == place, number, 0) for number, place in enumerate(places))
    chosen = sum(jnp.where(me_s == place, 1, 0) for place in places)
    owns = side * chosen == 1

    here = [(a, b) for a in range(outer) for b in range(inner)]
    here.sort(key=lambda step: hops(step, sizes), reverse=True)
    along_z = sorted(range(1, n_z), key=lambda step: ring_hops(step, n_z), reverse=True)
    ring = [(a, b) for a in (0, 1, n_grp - 1) for b in (0, 1, n_sub - 1) if (a, b) != (0, 0)]

    load_res = pltpu.make_async_copy(res_hbm, res_ref, load1)
    load_spacing = pltpu.make_async_copy(spacing_hbm, spacing_ref, load2)
    load_res.start()
    load_spacing.start()
    barrier = pltpu.get_barrier_semaphore()

    def greet(device):
        pl.semaphore_signal(barrier, inc=1, device_id=device, device_id_type=MESH)

    @pl.when(owns)
    def _():
        queue = [(hops(step, sizes), 0, step) for step in here]
        queue += [(hops(step, sizes), 1, step) for step in here if step != (0, 0)]
        queue += [(ring_hops(step, n_z), 2, step) for step in along_z]
        for _, kind, step in sorted(queue, reverse=True):
            if kind == 2:
                greet((2 * ((me_z + step) % n_z) + 1, me_s))
            else:
                greet((owner_g if kind else other_g, moved(step)))

    @pl.when(jnp.logical_not(owns))
    def _():
        for place in places:
            greet((owner_g, place))

    for a, b in ring:
        greet(((me_g + a) % n_grp, (me_s + b) % n_sub))

    shape_t = (n_sub, LANES)
    owner = iota(shape_t, 0)
    second_half = lax.broadcasted_iota(jnp.int32, shape_t, 1) >= HALF
    alone = owner == 0.0
    wave = jnp.where(alone & second_half, 1.0 * n_sub, owner)
    shift = jnp.where(second_half & jnp.logical_not(alone), 0.25 * nx5, 0.0)
    for j in range(4):
        column = wrapped((2 * me_s + (j - 1)).astype(jnp.float32), nx5)
        table[j] = cos_turn(wrapped(wave * column - shift, nx5), nx5)

    load_spacing.wait()
    lane = lax.broadcasted_iota(jnp.int32, (8, LANES), 1)
    height8 = jnp.broadcast_to(spacing_ref[...], (8, LANES))
    face = 2.0 / (height8 + up_z(height8))
    upper8 = jnp.where(lane < LANES - 1, face, 0.0)
    lower8 = jnp.where(lane > 0, down_z(face), 0.0)
    diag8 = 4.0 * height8 + upper8 + lower8
    damp8 = DAMPING / diag8
    coef8 = (height8[None], upper8[None], lower8[None], diag8[None])

    pad[...] = jnp.zeros_like(pad)
    load_res.wait()
    pad[2:6, 2:6, :] = res_ref[...]
    block = pad[...]
    zero_row = jnp.zeros((1, 8, LANES), jnp.float32)

    def operate_zero(rows):
        south = jnp.concatenate([zero_row, rows[:-1]], 0)
        north = jnp.concatenate([rows[1:], zero_row], 0)
        return operate(rows, south, north, coef8)

    first = damp8[None] * block
    second = first + damp8[None] * (block - operate_zero(first))
    leftover = block - operate_zero(second)
    row_pairs = jnp.concatenate([leftover[2 * j] + leftover[2 * j + 1] for j in range(4)], 0)
    z_in = lax.broadcasted_iota(jnp.int32, (LANES, LANES), 0)
    z_out = lax.broadcasted_iota(jnp.int32, (LANES, LANES), 1)
    gather_z = jnp.where((z_in >> 1) == (z_out & (HALF - 1)), 1.0, 0.0)
    pairs[0:32, :] = matmul(row_pairs, 0.25 * gather_z)
    parts = [
        pairs[pl.ds(2 * j, 4, stride=8), :] + pairs[pl.ds(2 * j + 1, 4, stride=8), :]
        for j in range(4)
    ]
    for k in range(n_sub):
        total = table[0, k : k + 1, :] * parts[0]
        for j in range(1, 4):
            total = total + table[j, k : k + 1, :] * parts[j]
        msg1[k // 2, 4 * (k % 2) : 4 * (k % 2) + 4, :] = total

    spread_ref[...] = jnp.where((z_out >> 1) == (z_in & (HALF - 1)), 1.0, 0.0)

    pl.semaphore_wait(barrier, 8 + jnp.where(owns, 2 * n_sub - 1 + n_z - 1, n_own))

    def share(number, place):
        pltpu.make_async_remote_copy(
            src_ref=msg1.at[number], dst_ref=recv1.at[side * n_sub + me_s],
            send_sem=send1, recv_sem=got1,
            device_id=(owner_g, place), device_id_type=MESH,
        ).start()

    behind = (0.0, 0.4, 0.8, 1.2, 1.8, 1.7, 1.3, 1.1)

    def start_of(item):
        return 0.6 * ring_hops(item[1] // inner, outer) + behind[item[1] % 8]

    for number, place in sorted(enumerate(places), key=start_of, reverse=True):
        pl.when(jnp.logical_not(owns) | (me_s != place))(functools.partial(share, number, place))

    for place, (a, b) in enumerate(ring):
        pltpu.make_async_remote_copy(
            src_ref=res_ref, dst_ref=halo.at[place], send_sem=halo_send, recv_sem=halo_recv,
            device_id=((me_g + a) % n_grp, (me_s + b) % n_sub), device_id_type=MESH,
        ).start()

    height5 = matmul(height8, gather_z)

    @pl.when(owns)
    def _():
        recv1[n_sub + me_s] = msg1[own_index]
        transforms(n_grp, forward_ref, backward_ref)
        for pair in range(2):
            wave_f = (2 * own_index + pair).astype(jnp.float32)
            solve_modes(
                n_grp, n_sub, wave_f, height5, weights_z.at[pair], still_ref.at[pair]
            )
        arrived(recv1.at[pl.ds(0, 2 * n_sub - 1)], got1)
        other = jnp.sum(recv1[0:n_sub], axis=0)
        own = jnp.sum(recv1[n_sub : 2 * n_sub], axis=0)
        gap = jnp.zeros((2, LANES), jnp.float32)
        for pair in range(2):
            left, right = other[4 * pair : 4 * pair + 4], own[4 * pair : 4 * pair + 4]
            both = jnp.concatenate([left, gap, gap], 0) + jnp.concatenate([gap, right, gap], 0)
            msg2[pair] = both
            recv2[0, pair] = both
        for step in along_z:
            pltpu.make_async_remote_copy(
                src_ref=msg2, dst_ref=recv2.at[-step % n_z], send_sem=send2, recv_sem=got2,
                device_id=(2 * ((me_z + step) % n_z) + 1, me_s), device_id_type=MESH,
            ).start()
        arrived(recv2.at[pl.ds(1, n_z - 1)], got2)

        fields, means = [], []
        low_half = lax.broadcasted_iota(jnp.int32, (1, LANES), 1) < HALF
        rows_in = jnp.concatenate(
            [
                jnp.concatenate([recv2[k, pair] for k in range(n_z)], 0)
                for pair in range(2)
            ],
            1,
        )
        spectrum = matmul(forward_ref[...], rows_in)
        for pair in range(2):
            half = slice(LANES * pair, LANES * (pair + 1))
            fields.append(spectrum[:, half])
            column = jnp.where(low_half, jnp.sum(rows_in[:, half], axis=0, keepdims=True), 0.0)
            means.append(jnp.sum(column, axis=1, keepdims=True) * (1.0 / HALF))
        lines = [[], []]
        for pair in range(2):
            field = fields[pair] - still_ref[pair] * means[pair]
            for group in range(2):
                total = weights_z[pair, group, REACH] * field
                for offset in range(1, REACH + 1):
                    step = offset << (3 * group)
                    total = total + (
                        weights_z[pair, group, REACH - offset] * pltpu.roll(field, step, axis=1)
                        + weights_z[pair, group, REACH + offset]
                        * pltpu.roll(field, LANES - step, axis=1)
                    )
                field = total
            for r in range(6):
                line = backward_ref[r, 0:8] * field[0:8]
                for k in range(8, ny5, 8):
                    line = line + backward_ref[r, k : k + 8] * field[k : k + 8]
                lines[pair].append(jnp.sum(line, axis=0, keepdims=True))
        for core, first in ((0, 0), (1, 2)):
            msg3[core] = jnp.concatenate(
                lines[0][first : first + 4] + lines[1][first : first + 4], 0
            )
        recv3[own_index] = msg3[1]

        def give(core, place):
            pltpu.make_async_remote_copy(
                src_ref=msg3.at[core], dst_ref=recv3.at[own_index],
                send_sem=send3, recv_sem=got3,
                device_id=(owner_g if core else other_g, place), device_id_type=MESH,
            ).start()

        in_order = sorted(range(n_sub), key=lambda p: hops((p // inner, p % inner), sizes))
        for place in in_order:
            pl.when(me_s != place)(functools.partial(give, 1, place))
            give(0, place)

    for j in range(4):
        for number in range(n_own):
            table8[j, number] = jnp.concatenate(
                [
                    jnp.broadcast_to(table[j, k : k + 1, :], (4, LANES))
                    for k in (2 * number, 2 * number + 1)
                ],
                0,
            )

    arrived(halo, halo_recv)
    big[:, 12:16, :] = jnp.zeros((12, 4, LANES), jnp.float32)
    big[4:8, 4:8, :] = res_ref[...]
    for place, (a, b) in enumerate(ring):
        at_y = {0: 4, 1: 0, n_grp - 1: 8}[a]
        at_x = {0: 4, 1: 0, n_sub - 1: 8}[b]
        big[at_y : at_y + 4, at_x : at_x + 4, :] = halo[place]
    wide = big[...]
    coef1 = tuple(value[:, 0:1] for value in coef8)
    damp1 = damp8[None, 0:1]
    first_w = damp1 * wide
    inner_w = first_w[1:-1] + damp1 * (
        wide[1:-1] - operate(first_w[1:-1], first_w[:-2], first_w[2:], coef1)
    )
    smooth_ref[...] = inner_w[1:-1]
    smooth = smooth_ref[:, 2:10, :]
    near = big[2:10, 2:10, :]

    @pl.when(owns)
    def _():
        arrived(recv3.at[pl.ds(0, n_own - 1)], got3)

    @pl.when(jnp.logical_not(owns))
    def _():
        arrived(recv3, got3)

    for j in range(4):
        total = table8[j, 0] * recv3[0]
        for k in range(1, n_own):
            total = total + table8[j, k] * recv3[k]
        total = total[0:4] + total[4:8]
        pairs[pl.ds(2 * j, 4, stride=8), :] = total
        pairs[pl.ds(2 * j + 1, 4, stride=8), :] = total
    for j in (1, 2):
        both = pairs[pl.ds(8 * j + 2, 2, stride=2), :]
        coarse_ref[j - 1] = (both + pltpu.roll(both, HALF, axis=1))[:, 0:HALF]
    coarse = matmul(pairs[0:32, :], spread_ref[...])
    lifted = smooth + jnp.concatenate(
        [coarse[8 * (j // 2) : 8 * (j // 2) + 8][None] for j in range(8)], 0
    )
    lifted = lifted[1:-1] + damp8[None] * (
        near[1:-1] - operate(lifted[1:-1], lifted[:-2], lifted[2:], coef8)
    )
    lifted = lifted[1:-1] + damp8[None] * (
        near[2:-2] - operate(lifted[1:-1], lifted[:-2], lifted[2:], coef8)
    )
    cor_ref[...] = lifted[:, 2:6, :]

    arrived(halo, halo_send)

    @pl.when(owns)
    def _():
        arrived(recv1.at[pl.ds(0, n_own - 1)], send1)
        arrived(recv2.at[pl.ds(1, n_z - 1)], send2)
        arrived(recv1.at[pl.ds(0, 2 * n_sub - 1)], send3)

    @pl.when(jnp.logical_not(owns))
    def _():
        arrived(recv1.at[pl.ds(0, n_own)], send1)


def hand_over(cor_in, coarse_in, cor_out, coarse_out, sem1, sem2):
    first = pltpu.make_async_copy(cor_in, cor_out, sem1)
    second = pltpu.make_async_copy(coarse_in, coarse_out, sem2)
    first.start()
    second.start()
    first.wait()
    second.wait()


def on_device(n_grp, n_sub, residual4, spacing):
    f32 = jnp.float32
    ny5 = 2 * n_grp
    dma = pltpu.SemaphoreType.DMA
    vmem = pl.BlockSpec(memory_space=pltpu.VMEM)
    anywhere = pl.BlockSpec(memory_space=pl.ANY)
    correction, coarse = pl.pallas_call(
        functools.partial(kernel, n_grp, n_sub),
        out_shape=(
            pltpu.VMEM((4, 4, LANES), f32),
            pltpu.VMEM((2, 2, HALF), f32),
        ),
        in_specs=[anywhere, anywhere],
        out_specs=(vmem, vmem),
        scratch_shapes=[
            pltpu.VMEM((4, 4, LANES), f32),
            pltpu.VMEM((1, LANES), f32),
            pltpu.VMEM((8, 8, LANES), f32),
            pltpu.VMEM((4, n_sub, LANES), f32),
            pltpu.VMEM((4, n_sub // 2, 8, LANES), f32),
            pltpu.VMEM((n_sub // 2, 8, LANES), f32),
            pltpu.VMEM((2 * n_sub, 8, LANES), f32),
            pltpu.VMEM((2, 8, LANES), f32),
            pltpu.VMEM((n_grp // 2, 2, 8, LANES), f32),
            pltpu.VMEM((2, 8, LANES), f32),
            pltpu.VMEM((n_sub // 2, 8, LANES), f32),
            pltpu.VMEM((8, 4, 4, LANES), f32),
            pltpu.VMEM((12, 16, LANES), f32),
            pltpu.VMEM((8, 16, LANES), f32),
            pltpu.VMEM((80, LANES), f32),
            pltpu.VMEM((2, 2, 2 * REACH + 1, ny5, LANES), f32),
            pltpu.VMEM((ny5, 4 * n_grp), f32),
            pltpu.VMEM((6, ny5, LANES), f32),
            pltpu.VMEM((2, ny5, LANES), f32),
            pltpu.VMEM((LANES, LANES), f32),
        ]
        + [dma] * 10,
        compiler_params=pltpu.CompilerParams(collective_id=0, has_side_effects=True),
    )(jnp.transpose(residual4, (1, 2, 0)), spacing.reshape(1, LANES))
    correction, coarse = pl.pallas_call(
        hand_over,
        out_shape=(
            jax.ShapeDtypeStruct((4, 4, LANES), f32),
            jax.ShapeDtypeStruct((2, 2, HALF), f32),
        ),
        in_specs=[vmem, vmem],
        out_specs=(anywhere, anywhere),
        scratch_shapes=[dma] * 2,
    )(
        pltpu.with_memory_space_constraint(correction, pltpu.VMEM),
        pltpu.with_memory_space_constraint(coarse, pltpu.VMEM),
    )
    return jnp.transpose(correction, (2, 0, 1)), jnp.transpose(coarse, (2, 0, 1))


def solution(mesh):
    placed = P(None, "grp", "sub")
    return jax.shard_map(
        functools.partial(on_device, mesh.shape["grp"], mesh.shape["sub"]),
        mesh=mesh,
        in_specs=(placed, P()),
        out_specs=(placed, placed),
        check_vma=False,
    )
```

```python
import functools
import math

import jax
import jax.numpy as jnp
from jax import lax
from jax.experimental import pallas as pl
from jax.experimental.pallas import tpu as pltpu
from jax.sharding import PartitionSpec as P

MESH = pl.DeviceIdType.MESH
HIGHEST = lax.Precision.HIGHEST
DAMPING = 0.8
LANES = 128
HALF = 64
REACH = 7


def matmul(left, right):
    return lax.dot_general(
        left, right, (((1,), (0,)), ((), ())), precision=HIGHEST, preferred_element_type=jnp.float32
    )


def iota(shape, axis):
    return lax.broadcasted_iota(jnp.int32, shape, axis).astype(jnp.float32)


def wrapped(value, count):
    return value - count * jnp.floor((value + 0.5) * (1.0 / count))


def cos_turn(step, count):
    step = jnp.minimum(step, count - step)
    flip = step > count / 4
    step = jnp.where(flip, count / 2 - step, step)
    angle = step * (2.0 * math.pi / count)
    sq = angle * angle
    total = jnp.full_like(sq, 1.0 / math.factorial(16))
    for power in range(14, -1, -2):
        sign = 1.0 if power % 4 == 0 else -1.0
        total = total * sq + sign / math.factorial(power)
    return jnp.where(flip, -total, total)


def up_z(field):
    return pltpu.roll(field, LANES - 1, axis=field.ndim - 1)


def down_z(field):
    return pltpu.roll(field, 1, axis=field.ndim - 1)


def operate(rows, south, north, coef):
    height, upper, lower, diagonal = coef
    span = rows.shape[1]
    west = pltpu.roll(rows, 1, axis=1)
    east = pltpu.roll(rows, span - 1, axis=1)
    sides = (west + east) + (south + north)
    return diagonal * rows - height * sides - upper * up_z(rows) - lower * down_z(rows)


def torus(n_sub):
    inner = 8 if n_sub % 8 == 0 else 2
    return n_sub // inner, inner


def ring_hops(step, size):
    return min(step % size, -step % size)


def hops(step, sizes):
    return ring_hops(step[0], sizes[0]) + ring_hops(step[1], sizes[1])


def compose(weights, keep, down, up, step):
    terms = {}
    for offset, weight in weights.items():
        for place, part in (
            (offset, keep * weight),
            (offset - step, down * pltpu.roll(weight, step, axis=1)),
            (offset + step, up * pltpu.roll(weight, LANES - step, axis=1)),
        ):
            terms[place] = terms[place] + part if place in terms else part
    return terms


def owner_places(n_sub):
    outer, inner = torus(n_sub)

    def rank(place):
        step = (place // inner, place % inner)
        return hops(step, (outer, inner)), step[1]

    return sorted(range(n_sub), key=rank)[: n_sub // 2]


def arrived(blocks, semaphore):
    pltpu.make_async_copy(blocks, blocks, semaphore).wait()


def solve_modes(n_grp, n_sub, wave_f, height5, weights_z, still_ref):
    ny5, nx5 = 2 * n_grp, 2 * n_sub
    lane_m = lax.broadcasted_iota(jnp.int32, (ny5, LANES), 1)
    row_m = lax.broadcasted_iota(jnp.int32, (ny5, LANES), 0)
    z5 = lane_m & (HALF - 1)
    z5_8 = z5[0:8]
    face5 = 2.0 / (height5 + up_z(height5))
    upper5 = jnp.where(z5_8 < HALF - 1, face5, 0.0)[0:1]
    lower5 = jnp.where(z5_8 > 0, down_z(face5), 0.0)[0:1]
    height5 = height5[0:1]
    mode = row_m.astype(jnp.float32)
    odd = mode > n_grp
    wave_y = jnp.where(odd, mode - n_grp, mode)
    sin_y = cos_turn(n_grp - wave_y, 2 * ny5)
    wave_x = jnp.where((lane_m >= HALF) & (wave_f == 0.0), 1.0 * n_sub, wave_f)
    sin_x = cos_turn(n_sub - wave_x, 2 * nx5)
    lam = sin_x * sin_x + sin_y * sin_y
    still = (row_m == 0) & (wave_x == 0.0)
    still_ref[...] = jnp.where(still, 1.0, 0.0)
    anchor = jnp.where(still & (z5 == 0), 1.0, 0.0)
    excess = lam * height5 + anchor
    inverse = 1.0 / (excess + upper5 + lower5)
    below = lower5 * inverse
    above = upper5 * inverse
    excess = excess * inverse
    weight = jnp.where(wave_f == 0.0, 1.0 / nx5, 2.0 / nx5)
    terms = {0: inverse}
    for level in range(6):
        step = 1 << level
        below_dn = pltpu.roll(below, step, axis=1)
        above_up = pltpu.roll(above, LANES - step, axis=1)
        excess_dn = pltpu.roll(excess, step, axis=1)
        excess_up = pltpu.roll(excess, LANES - step, axis=1)
        inverse = 1.0 / (excess + below * (below_dn + excess_dn) + above * (above_up + excess_up))
        low, high = below * inverse, above * inverse
        last = weight if level == 5 else 1.0
        keep, down, up = inverse * last, low * last, high * last
        terms = (
            {0: keep, -step: down, step: up} if level == 3 else compose(terms, keep, down, up, step)
        )
        if level % 3 == 2:
            for offset in range(-REACH, REACH + 1):
                weights_z[level // 3, REACH + offset] = terms[offset * (step >> 2)]
        excess = excess * inverse + low * excess_dn + high * excess_up
        below, above = low * below_dn, high * above_up


def transforms(n_grp, forward_ref, backward_ref):
    ny5 = 2 * n_grp
    mode = iota((ny5, LANES), 0)
    odd = mode > n_grp
    wave_y = jnp.where(odd, mode - n_grp, mode)
    shape_f = (ny5, 4 * n_grp)
    mode_f, col_f = iota(shape_f, 0), iota(shape_f, 1)
    chip_f = jnp.floor((col_f + 0.5) * 0.125)
    row_f = wrapped(4.0 * chip_f + (col_f - 8.0 * chip_f) - 1.0, ny5)
    odd_f = mode_f > n_grp
    phase_f = jnp.where(odd_f, mode_f - n_grp, mode_f) * row_f - jnp.where(odd_f, 0.25 * ny5, 0.0)
    forward_ref[...] = cos_turn(wrapped(phase_f, ny5), ny5)
    scale = jnp.where((wave_y == 0.0) | (wave_y == 1.0 * n_grp), 1.0 / ny5, 2.0 / ny5)
    quarter = jnp.where(odd, 0.25 * ny5, 0.0)
    for r in range(6):
        backward_ref[r] = cos_turn(wrapped(wave_y * (r - 1.0) - quarter, ny5), ny5) * scale


def kernel(
    n_grp, n_sub,
    res_hbm, spacing_hbm, cor_ref, coarse_ref,
    res_ref, spacing_ref, pad, table, table8, msg1, recv1, msg2, recv2, msg3, recv3, halo, big, smooth_ref,
    pairs, weights_z, forward_ref, backward_ref, still_ref, spread_ref,
    load1, load2, halo_send, halo_recv, send1, got1, send2, got2, send3, got3,
):
    me_g = lax.axis_index("grp")
    me_s = lax.axis_index("sub")
    ny5, nx5 = 2 * n_grp, 2 * n_sub
    n_z = n_grp // 2
    sizes = torus(n_sub)
    outer, inner = sizes
    me_z, side = me_g // 2, me_g % 2
    owner_g, other_g = 2 * me_z + 1, 2 * me_z

    def moved(step):
        return ((me_s // inner + step[0]) % outer) * inner + (me_s % inner + step[1]) % inner

    places = owner_places(n_sub)
    n_own = len(places)
    own_index = sum(jnp.where(me_s == place, number, 0) for number, place in enumerate(places))
    chosen = sum(jnp.where(me_s == place, 1, 0) for place in places)
    owns = side * chosen == 1

    here = [(a, b) for a in range(outer) for b in range(inner)]
    here.sort(key=lambda step: hops(step, sizes), reverse=True)
    along_z = sorted(range(1, n_z), key=lambda step: ring_hops(step, n_z), reverse=True)
    ring = [(a, b) for a in (0, 1, n_grp - 1) for b in (0, 1, n_sub - 1) if (a, b) != (0, 0)]

    load_res = pltpu.make_async_copy(res_hbm, res_ref, load1)
    load_spacing = pltpu.make_async_copy(spacing_hbm, spacing_ref, load2)
    load_res.start()
    load_spacing.start()
    barrier = pltpu.get_barrier_semaphore()

    def greet(device):
        pl.semaphore_signal(barrier, inc=1, device_id=device, device_id_type=MESH)

    @pl.when(owns)
    def _():
        queue = [(hops(step, sizes), 0, step) for step in here]
        queue += [(hops(step, sizes), 1, step) for step in here if step != (0, 0)]
        queue += [(ring_hops(step, n_z), 2, step) for step in along_z]
        for _, kind, step in sorted(queue, reverse=True):
            if kind == 2:
                greet((2 * ((me_z + step) % n_z) + 1, me_s))
            else:
                greet((owner_g if kind else other_g, moved(step)))

    @pl.when(jnp.logical_not(owns))
    def _():
        for place in places:
            greet((owner_g, place))

    for a, b in ring:
        greet(((me_g + a) % n_grp, (me_s + b) % n_sub))

    shape_t = (n_sub, LANES)
    owner = iota(shape_t, 0)
    second_half = lax.broadcasted_iota(jnp.int32, shape_t, 1) >= HALF
    alone = owner == 0.0
    wave = jnp.where(alone & second_half, 1.0 * n_sub, owner)
    shift = jnp.where(second_half & jnp.logical_not(alone), 0.25 * nx5, 0.0)
    for j in range(4):
        column = wrapped((2 * me_s + (j - 1)).astype(jnp.float32), nx5)
        table[j] = cos_turn(wrapped(wave * column - shift, nx5), nx5)

    load_spacing.wait()
    lane = lax.broadcasted_iota(jnp.int32, (8, LANES), 1)
    height8 = jnp.broadcast_to(spacing_ref[...], (8, LANES))
    face = 2.0 / (height8 + up_z(height8))
    upper8 = jnp.where(lane < LANES - 1, face, 0.0)
    lower8 = jnp.where(lane > 0, down_z(face), 0.0)
    diag8 = 4.0 * height8 + upper8 + lower8
    damp8 = DAMPING / diag8
    coef8 = (height8[None], upper8[None], lower8[None], diag8[None])

    pad[...] = jnp.zeros_like(pad)
    load_res.wait()
    pad[2:6, 2:6, :] = res_ref[...]
    block = pad[...]
    zero_row = jnp.zeros((1, 8, LANES), jnp.float32)

    def operate_zero(rows):
        south = jnp.concatenate([zero_row, rows[:-1]], 0)
        north = jnp.concatenate([rows[1:], zero_row], 0)
        return operate(rows, south, north, coef8)

    first = damp8[None] * block
    second = first + damp8[None] * (block - operate_zero(first))
    leftover = block - operate_zero(second)
    row_pairs = jnp.concatenate([leftover[2 * j] + leftover[2 * j + 1] for j in range(4)], 0)
    z_in = lax.broadcasted_iota(jnp.int32, (LANES, LANES), 0)
    z_out = lax.broadcasted_iota(jnp.int32, (LANES, LANES), 1)
    gather_z = jnp.where((z_in >> 1) == (z_out & (HALF - 1)), 1.0, 0.0)
    pairs[0:32, :] = matmul(row_pairs, 0.25 * gather_z)
    parts = [
        pairs[pl.ds(2 * j, 4, stride=8), :] + pairs[pl.ds(2 * j + 1, 4, stride=8), :]
        for j in range(4)
    ]
    for k in range(n_sub):
        total = table[0, k : k + 1, :] * parts[0]
        for j in range(1, 4):
            total = total + table[j, k : k + 1, :] * parts[j]
        msg1[k // 2, 4 * (k % 2) : 4 * (k % 2) + 4, :] = total

    spread_ref[...] = jnp.where((z_out >> 1) == (z_in & (HALF - 1)), 1.0, 0.0)

    pl.semaphore_wait(barrier, 8 + jnp.where(owns, 2 * n_sub - 1 + n_z - 1, n_own))

    def share(number, place):
        pltpu.make_async_remote_copy(
            src_ref=msg1.at[number], dst_ref=recv1.at[side * n_sub + me_s],
            send_sem=send1, recv_sem=got1,
            device_id=(owner_g, place), device_id_type=MESH,
        ).start()

    behind = (0.0, 0.4, 0.8, 1.2, 1.8, 1.7, 1.3, 1.1)

    def start_of(item):
        return 0.6 * ring_hops(item[1] // inner, outer) + behind[item[1] % 8]

    for number, place in sorted(enumerate(places), key=start_of, reverse=True):
        pl.when(jnp.logical_not(owns) | (me_s != place))(functools.partial(share, number, place))

    for place, (a, b) in enumerate(ring):
        pltpu.make_async_remote_copy(
            src_ref=res_ref, dst_ref=halo.at[place], send_sem=halo_send, recv_sem=halo_recv,
            device_id=((me_g + a) % n_grp, (me_s + b) % n_sub), device_id_type=MESH,
        ).start()

    height5 = matmul(height8, gather_z)

    @pl.when(owns)
    def _():
        recv1[n_sub + me_s] = msg1[own_index]
        transforms(n_grp, forward_ref, backward_ref)
        for pair in range(2):
            wave_f = (2 * own_index + pair).astype(jnp.float32)
            solve_modes(
                n_grp, n_sub, wave_f, height5, weights_z.at[pair], still_ref.at[pair]
            )
        arrived(recv1.at[pl.ds(0, 2 * n_sub - 1)], got1)
        other = jnp.sum(recv1[0:n_sub], axis=0)
        own = jnp.sum(recv1[n_sub : 2 * n_sub], axis=0)
        gap = jnp.zeros((2, LANES), jnp.float32)
        for pair in range(2):
            left, right = other[4 * pair : 4 * pair + 4], own[4 * pair : 4 * pair + 4]
            both = jnp.concatenate([left, gap, gap], 0) + jnp.concatenate([gap, right, gap], 0)
            msg2[pair] = both
            recv2[0, pair] = both
        def pass_on(plane):
            pltpu.make_async_remote_copy(
                src_ref=msg2, dst_ref=recv2.at[(me_z - plane + n_z) % n_z],
                send_sem=send2, recv_sem=got2,
                device_id=(2 * plane + 1, me_s), device_id_type=MESH,
            ).start()

        for plane in range(n_z):
            pl.when(me_z != plane)(functools.partial(pass_on, plane))
        arrived(recv2.at[pl.ds(1, n_z - 1)], got2)

        fields, means = [], []
        low_half = lax.broadcasted_iota(jnp.int32, (1, LANES), 1) < HALF
        rows_in = jnp.concatenate(
            [
                jnp.concatenate([recv2[k, pair] for k in range(n_z)], 0)
                for pair in range(2)
            ],
            1,
        )
        spectrum = matmul(forward_ref[...], rows_in)
        for pair in range(2):
            half = slice(LANES * pair, LANES * (pair + 1))
            fields.append(spectrum[:, half])
            column = jnp.where(low_half, jnp.sum(rows_in[:, half], axis=0, keepdims=True), 0.0)
            means.append(jnp.sum(column, axis=1, keepdims=True) * (1.0 / HALF))
        lines = [[], []]
        for pair in range(2):
            field = fields[pair] - still_ref[pair] * means[pair]
            for group in range(2):
                total = weights_z[pair, group, REACH] * field
                for offset in range(1, REACH + 1):
                    step = offset << (3 * group)
                    total = total + (
                        weights_z[pair, group, REACH - offset] * pltpu.roll(field, step, axis=1)
                        + weights_z[pair, group, REACH + offset]
                        * pltpu.roll(field, LANES - step, axis=1)
                    )
                field = total
            for r in range(6):
                line = backward_ref[r, 0:8] * field[0:8]
                for k in range(8, ny5, 8):
                    line = line + backward_ref[r, k : k + 8] * field[k : k + 8]
                lines[pair].append(jnp.sum(line, axis=0, keepdims=True))
        for core, first in ((0, 0), (1, 2)):
            msg3[core] = jnp.concatenate(
                lines[0][first : first + 4] + lines[1][first : first + 4], 0
            )
        recv3[own_index] = msg3[1]

        def give(core, place):
            pltpu.make_async_remote_copy(
                src_ref=msg3.at[core], dst_ref=recv3.at[own_index],
                send_sem=send3, recv_sem=got3,
                device_id=(owner_g if core else other_g, place), device_id_type=MESH,
            ).start()

        in_order = sorted(range(n_sub), key=lambda p: hops((p // inner, p % inner), sizes))
        for place in in_order:
            pl.when(me_s != place)(functools.partial(give, 1, place))
            give(0, place)

    for j in range(4):
        for number in range(n_own):
            table8[j, number] = jnp.concatenate(
                [
                    jnp.broadcast_to(table[j, k : k + 1, :], (4, LANES))
                    for k in (2 * number, 2 * number + 1)
                ],
                0,
            )

    arrived(halo, halo_recv)
    big[:, 12:16, :] = jnp.zeros((12, 4, LANES), jnp.float32)
    big[4:8, 4:8, :] = res_ref[...]
    for place, (a, b) in enumerate(ring):
        at_y = {0: 4, 1: 0, n_grp - 1: 8}[a]
        at_x = {0: 4, 1: 0, n_sub - 1: 8}[b]
        big[at_y : at_y + 4, at_x : at_x + 4, :] = halo[place]
    wide = big[...]
    coef1 = tuple(value[:, 0:1] for value in coef8)
    damp1 = damp8[None, 0:1]
    first_w = damp1 * wide
    inner_w = first_w[1:-1] + damp1 * (
        wide[1:-1] - operate(first_w[1:-1], first_w[:-2], first_w[2:], coef1)
    )
    smooth_ref[...] = inner_w[1:-1]
    smooth = smooth_ref[:, 2:10, :]
    near = big[2:10, 2:10, :]

    @pl.when(owns)
    def _():
        arrived(recv3.at[pl.ds(0, n_own - 1)], got3)

    @pl.when(jnp.logical_not(owns))
    def _():
        arrived(recv3, got3)

    for j in range(4):
        total = table8[j, 0] * recv3[0]
        for k in range(1, n_own):
            total = total + table8[j, k] * recv3[k]
        total = total[0:4] + total[4:8]
        pairs[pl.ds(2 * j, 4, stride=8), :] = total
        pairs[pl.ds(2 * j + 1, 4, stride=8), :] = total
    for j in (1, 2):
        both = pairs[pl.ds(8 * j + 2, 2, stride=2), :]
        coarse_ref[j - 1] = (both + pltpu.roll(both, HALF, axis=1))[:, 0:HALF]
    coarse = matmul(pairs[0:32, :], spread_ref[...])
    lifted = smooth + jnp.concatenate(
        [coarse[8 * (j // 2) : 8 * (j // 2) + 8][None] for j in range(8)], 0
    )
    lifted = lifted[1:-1] + damp8[None] * (
        near[1:-1] - operate(lifted[1:-1], lifted[:-2], lifted[2:], coef8)
    )
    lifted = lifted[1:-1] + damp8[None] * (
        near[2:-2] - operate(lifted[1:-1], lifted[:-2], lifted[2:], coef8)
    )
    cor_ref[...] = lifted[:, 2:6, :]

    arrived(halo, halo_send)

    @pl.when(owns)
    def _():
        arrived(recv1.at[pl.ds(0, n_own - 1)], send1)
        arrived(recv2.at[pl.ds(1, n_z - 1)], send2)
        arrived(recv1.at[pl.ds(0, 2 * n_sub - 1)], send3)

    @pl.when(jnp.logical_not(owns))
    def _():
        arrived(recv1.at[pl.ds(0, n_own)], send1)


def hand_over(cor_in, coarse_in, cor_out, coarse_out, sem1, sem2):
    first = pltpu.make_async_copy(cor_in, cor_out, sem1)
    second = pltpu.make_async_copy(coarse_in, coarse_out, sem2)
    first.start()
    second.start()
    first.wait()
    second.wait()


def on_device(n_grp, n_sub, residual4, spacing):
    f32 = jnp.float32
    ny5 = 2 * n_grp
    dma = pltpu.SemaphoreType.DMA
    vmem = pl.BlockSpec(memory_space=pltpu.VMEM)
    anywhere = pl.BlockSpec(memory_space=pl.ANY)
    correction, coarse = pl.pallas_call(
        functools.partial(kernel, n_grp, n_sub),
        out_shape=(
            pltpu.VMEM((4, 4, LANES), f32),
            pltpu.VMEM((2, 2, HALF), f32),
        ),
        in_specs=[anywhere, anywhere],
        out_specs=(vmem, vmem),
        scratch_shapes=[
            pltpu.VMEM((4, 4, LANES), f32),
            pltpu.VMEM((1, LANES), f32),
            pltpu.VMEM((8, 8, LANES), f32),
            pltpu.VMEM((4, n_sub, LANES), f32),
            pltpu.VMEM((4, n_sub // 2, 8, LANES), f32),
            pltpu.VMEM((n_sub // 2, 8, LANES), f32),
            pltpu.VMEM((2 * n_sub, 8, LANES), f32),
            pltpu.VMEM((2, 8, LANES), f32),
            pltpu.VMEM((n_grp // 2, 2, 8, LANES), f32),
            pltpu.VMEM((2, 8, LANES), f32),
            pltpu.VMEM((n_sub // 2, 8, LANES), f32),
            pltpu.VMEM((8, 4, 4, LANES), f32),
            pltpu.VMEM((12, 16, LANES), f32),
            pltpu.VMEM((8, 16, LANES), f32),
            pltpu.VMEM((80, LANES), f32),
            pltpu.VMEM((2, 2, 2 * REACH + 1, ny5, LANES), f32),
            pltpu.VMEM((ny5, 4 * n_grp), f32),
            pltpu.VMEM((6, ny5, LANES), f32),
            pltpu.VMEM((2, ny5, LANES), f32),
            pltpu.VMEM((LANES, LANES), f32),
        ]
        + [dma] * 10,
        compiler_params=pltpu.CompilerParams(collective_id=0, has_side_effects=True),
    )(jnp.transpose(residual4, (1, 2, 0)), spacing.reshape(1, LANES))
    correction, coarse = pl.pallas_call(
        hand_over,
        out_shape=(
            jax.ShapeDtypeStruct((4, 4, LANES), f32),
            jax.ShapeDtypeStruct((2, 2, HALF), f32),
        ),
        in_specs=[vmem, vmem],
        out_specs=(anywhere, anywhere),
        scratch_shapes=[dma] * 2,
    )(
        pltpu.with_memory_space_constraint(correction, pltpu.VMEM),
        pltpu.with_memory_space_constraint(coarse, pltpu.VMEM),
    )
    return jnp.transpose(correction, (2, 0, 1)), jnp.transpose(coarse, (2, 0, 1))


def solution(mesh):
    placed = P(None, "grp", "sub")
    return jax.shard_map(
        functools.partial(on_device, mesh.shape["grp"], mesh.shape["sub"]),
        mesh=mesh,
        in_specs=(placed, P()),
        out_specs=(placed, placed),
        check_vma=False,
    )
```
